256 devices in a mesh: expert: 64 (over y, z, core), half: 4 (over x).
Axes of the slice: x: 4, y: 4, z: 8, core: 2. Of those that a mesh axis runs over, the one named last changes fastest.
Arguments:
- tokens: bfloat16 [8192, 2048], P('expert', 'half'), may hold values from -6 to 6
- cotangent: bfloat16 [8192, 2048], P('expert', 'half'), may hold values from -4 to 4
- route: int32 [8192, 8], P('expert'), may hold values from 0 to 127, all different within a row; in each aligned block of 128 rows (0 to 127, 128 to 255, ...) at most 16 rows name the same one
- prob: bfloat16 [8192, 8], P('expert'), may hold values from 0.19921875 to 1
- w_gate: bfloat16 [128, 768, 2048], P('expert', 'half'), may hold values from -0.125 to 0.125
- w_up: bfloat16 [128, 768, 2048], P('expert', 'half'), may hold values from -0.125 to 0.125
- w_down: bfloat16 [128, 768, 2048], P('expert', 'half'), may hold values from -0.21875 to 0.21875
Outputs:
- grad_tokens: bfloat16 [8192, 2048], P('expert', 'half')
- grad_prob: float32 [8192, 8], P('expert')
- grad_gate: bfloat16 [128, 768, 2048], P('expert', 'half')
- grad_up: bfloat16 [128, 768, 2048], P('expert', 'half')
- grad_down: bfloat16 [128, 768, 2048], P('expert', 'half')
The draws below stay inside these ranges and needn't reach their ends.
Inputs may be any that keep to these rules, and one draw needn't show every extreme that they name: `route`: each row names 8 different experts; among the rows of one device no expert is named more than 16 times, and that most is reached.
All inputs are finite; a program needn't handle non-finite values.
Results may differ from the reference program's by a relative error of at most 0.013.
Values may be sent and summed in bfloat16 or wider, within the bound.
No kernel may reach another device: no remote copies, remote signals or barrier semaphores. Data moves between devices by JAX's collectives and lax.ppermute only.
A program may use at most 192 MiB of HBM per device.

```python
import math
import jax
import jax.numpy as jnp
import numpy as np
from jax import lax

D = 2048
FF = 768
K = 8
TOK_DEV = 128
E = 128
TOKENS = 8192
CAP = 16
N_EXPERT = 64
N_HALF = 4


def block_levels(key, extent, split, smallest, top_value):
    loudness, own = 1.0, jax.random.fold_in(key, 6)
    for position, blocks in split:
        steps = jnp.exp(jax.random.uniform(jax.random.fold_in(own, position), (blocks,), jnp.float32, smallest / len(split), top_value / len(split)))
        loudness = loudness * jnp.repeat(steps, extent[position] // blocks).reshape([-1 if axis == position else 1 for axis in range(len(extent))])
    return loudness


def shared_out(key, own, number, rows, number_of, top, limit, lean):
    order = jax.random.permutation(key, number_of)
    packed, usual = load_shares(number_of, rows * top, limit, lean, True), load_shares(number_of, rows * top, limit, lean, False)
    places = jnp.arange(number_of)

    def named(sizes, offset_by):
        used = int((sizes > 0).sum())
        fixed = max(1, used // 4)
        shifted = fixed + (places - fixed + offset_by * (used - fixed)) % max(1, number_of - fixed)
        return jnp.zeros((number_of,), jnp.int32).at[order[jnp.where(places < fixed, places, shifted)]].set(jnp.asarray(sizes, jnp.int32))

    sizes = jnp.where(number % 4 == 0, named(packed, number // 4), named(usual, number - number // 4 - 1))
    mixed = jax.random.permutation(jax.random.fold_in(own, 3), number_of)
    giver, sink = mixed[0:number_of // 2 * 2:2], mixed[1:number_of // 2 * 2:2]
    margin = jnp.minimum(sizes[giver] - 1, limit - sizes[sink]) // 2
    margin = jnp.where((giver == order[0]) | (sink == order[0]) | (sizes[sink] == 0), 0, jnp.maximum(margin, 0))
    shifted = jax.random.randint(jax.random.fold_in(own, 4), (number_of // 2,), 0, 1 << 20) % (margin + 1)
    sizes = sizes.at[giver].add(-shifted).at[sink].add(shifted)
    members = jnp.searchsorted(jnp.cumsum(sizes), jnp.arange(rows * top), side="right").astype(jnp.int32)
    table = members.reshape(top, rows).T
    table = table[jax.random.permutation(jax.random.fold_in(own, 1), rows)]
    offset_by = jax.random.randint(jax.random.fold_in(own, 2), (rows, 1), 0, top)
    return jnp.take_along_axis(table, (jnp.arange(top)[None, :] + offset_by) % top, axis=1)


def load_shares(number_of, total, reach, skew, full):
    loads = [(1 << 20) // math.isqrt(rank ** skew) + 1 for rank in range(1, number_of + 1)]
    largest = reach if full else min(reach, max(-(-total // number_of), total * loads[0] // sum(loads)))
    least = 1 if total - largest >= number_of - 1 else 0
    counts, rest = [largest] + [least] * (number_of - 1), total - largest - least * (number_of - 1)
    while rest > 0:
        movable = [i for i in range(1, number_of) if counts[i] < largest] or [i for i in range(1, number_of) if counts[i] < reach]
        whole, budget = sum([loads[i] for i in movable]), rest
        for i in movable:
            more = min(reach - counts[i], max(1, budget * loads[i] // whole), rest)
            counts[i] = counts[i] + more
            rest = rest - more
    return np.array(counts)


def bell_draw(rng, shape, scale, bound, split=(), kind=jnp.bfloat16):
    array = scale * jax.random.normal(rng, shape, jnp.float32)
    if split:
        array = array * block_levels(rng, shape, split, -0.22, 0.18)
    return jnp.clip(array, -bound, bound).astype(kind)


def setup_inputs(seed: int = 0) -> dict:
    key_of = jax.random.split(jax.random.key(seed), 8)
    tokens = bell_draw(key_of[0], (TOKENS, D), 1.0, 6.0, ((0, 64), (1, 4)))
    cotangent = bell_draw(key_of[1], (TOKENS, D), 0.5, 4.0, ((0, 64), (1, 4)))
    route_keys = jax.random.split(jax.random.fold_in(key_of[2], 1), TOKENS // TOK_DEV)
    route_turns = jax.random.permutation(jax.random.fold_in(key_of[2], 3), TOKENS // TOK_DEV)
    route = jax.vmap(lambda own, number: shared_out(jax.random.fold_in(key_of[2], 2), own, number, TOK_DEV, E, K, CAP, 2))(route_keys, route_turns).reshape((TOKENS, K))
    prob = jnp.clip(0.19921875 + 0.80078125 * jax.random.uniform(key_of[3], (TOKENS, K), jnp.float32) ** block_levels(key_of[3], (TOKENS, K), ((0, 64),), -0.2, 0.2), 0.19921875, 1.0).astype(jnp.bfloat16)
    w_gate = bell_draw(key_of[4], (E, FF, D), D ** -0.5, 0.125, ((0, 64), (1, 4)))
    w_up = bell_draw(key_of[5], (E, FF, D), D ** -0.5, 0.125, ((0, 64), (1, 4)))
    w_down = bell_draw(key_of[6], (E, FF, D), FF ** -0.5, 0.21875, ((0, 64), (1, 4)))
    return dict(tokens=tokens, cotangent=cotangent, route=route, prob=prob, w_gate=w_gate, w_up=w_up, w_down=w_down)


def reference(tokens, cotangent, route, prob, w_gate, w_up, w_down):
    flat_route = route.reshape(-1)
    flat_prob = prob.reshape(-1).astype(jnp.float32)
    rows_max = N_EXPERT * CAP
    count = TOKENS * K
    order = jnp.arange(count, dtype=jnp.int32)
    quarter = FF // N_HALF

    def one_expert(carry, expert):
        grad_in, grad_weight = carry
        chosen = flat_route == expert
        place = jnp.where(chosen, jnp.cumsum(chosen.astype(jnp.int32)) - 1, rows_max).astype(jnp.int32)
        source = jnp.zeros((rows_max,), jnp.int32).at[place].set(order, mode="drop")
        filled = jnp.zeros((rows_max,), jnp.float32).at[place].set(1.0, mode="drop")
        token_of = (source // K).astype(jnp.int32)
        keep = filled[:, None] > 0.5
        xin = jnp.where(keep, tokens[token_of], jnp.zeros((), jnp.bfloat16))
        dout = jnp.where(keep, cotangent[token_of], jnp.zeros((), jnp.bfloat16))
        weight = flat_prob[source] * filled
        wgate = w_gate[expert]
        wup = w_up[expert]
        wdown = w_down[expert]
        gate = jnp.dot(xin, wgate.T, preferred_element_type=jnp.float32)
        upval = jnp.dot(xin, wup.T, preferred_element_type=jnp.float32)
        sig = jax.nn.sigmoid(gate)
        act = gate * sig
        hidden = (act * upval).astype(jnp.bfloat16)
        raw = jnp.dot(dout, wdown.T, preferred_element_type=jnp.float32)
        score = jnp.sum(hidden.astype(jnp.float32) * raw, axis=1)
        scaled = (weight[:, None] * dout.astype(jnp.float32)).astype(jnp.bfloat16)
        dact = weight[:, None] * raw
        dgate = (dact * upval * sig * (1.0 + gate * (1.0 - sig))).astype(jnp.bfloat16)
        dup = (dact * act).astype(jnp.bfloat16)
        grad_down = jnp.dot(hidden.T, scaled, preferred_element_type=jnp.float32).astype(jnp.bfloat16)
        grad_gate = jnp.dot(dgate.T, xin, preferred_element_type=jnp.float32).astype(jnp.bfloat16)
        grad_up = jnp.dot(dup.T, xin, preferred_element_type=jnp.float32).astype(jnp.bfloat16)
        dgate_f = dgate.astype(jnp.float32).reshape(rows_max, N_HALF, quarter)
        dup_f = dup.astype(jnp.float32).reshape(rows_max, N_HALF, quarter)
        wgate_f = wgate.astype(jnp.float32).reshape(N_HALF, quarter, D)
        wup_f = wup.astype(jnp.float32).reshape(N_HALF, quarter, D)
        parts = jnp.einsum("rhf,hfd->hrd", dgate_f, wgate_f) + jnp.einsum("rhf,hfd->hrd", dup_f, wup_f)
        parts = parts.astype(jnp.bfloat16).astype(jnp.float32)
        part_sum = jnp.sum(parts, axis=0) * filled[:, None]
        grad_in = grad_in.at[token_of].add(part_sum)
        grad_weight = grad_weight.at[source].add(score * filled)
        return (grad_in, grad_weight), (grad_gate, grad_up, grad_down)

    start = (jnp.zeros((TOKENS, D), jnp.float32), jnp.zeros((count,), jnp.float32))
    (grad_in, grad_weight), (grad_gate, grad_up, grad_down) = lax.scan(one_expert, start, jnp.arange(E, dtype=jnp.int32))
    return grad_in.astype(jnp.bfloat16), grad_weight.reshape(TOKENS, K), grad_gate, grad_up, grad_down
```

```python
import jax
import jax.numpy as jnp
from jax import lax
from jax.sharding import Mesh, PartitionSpec as P

BF = jnp.bfloat16
F32 = jnp.float32
NY, NZ, NC, NX = 4, 8, 2, 4
SLOT = 16


def dot32(spec, a, b):
    return jnp.einsum(spec, a, b, preferred_element_type=F32)


def before(n):
    at = jnp.arange(n)
    return (at[:, None] < at[None, :]).astype(BF)


def weight_pairs(m):
    pairs = []
    for c in range(NC):
        for h in range(NX):
            k = (h + m) % 2
            pairs.append((c * NX + h, (h // 2) * NX + 2 * c + k))
    return pairs


def per_device(tokens, cotangent, route, prob, w_gate, w_up, w_down):
    iy, iz, ic, ix = (lax.axis_index(a) for a in ("y", "z", "c", "x"))
    tok_rows, top = route.shape
    quarter = tokens.shape[1]
    sib = [(0, 1), (1, 0)]

    with jax.named_scope("routing"):
        table = jnp.concatenate([route.T.astype(BF), prob.T], axis=0)
        table = lax.all_gather(table, ("y", "z", "c"), axis=0, tiled=False)
        table = table.reshape(NY, NZ, NC, 2 * top, tok_rows)

    with jax.named_scope("gather_z"):
        xz = lax.all_gather(tokens, "z", axis=0, tiled=False)
        dz = lax.all_gather(cotangent, "z", axis=0, tiled=False)

    with jax.named_scope("weights_out"):
        wparts = []
        for m in range(2):
            k = (ix + m) % 2
            piece = jnp.stack([lax.dynamic_index_in_dim(w, k, 0, keepdims=False) for w in (w_gate, w_up, w_down)])
            wparts.append(lax.ppermute(piece, ("c", "x"), weight_pairs(m)))
        weights = jnp.concatenate(wparts, axis=1)
        wg, wu, wd = weights[0], weights[1], weights[2]

    with jax.named_scope("select"):
        mid = lax.dynamic_index_in_dim(table, iy, 0, keepdims=False)
        mid = lax.dynamic_index_in_dim(mid, ic, 1, keepdims=False)
        ids = 4 * (jnp.arange(NY)[:, None] * NZ + iz) + jnp.arange(NX)[None, :]
        ids = ids.reshape(-1).astype(BF)
        hit = jnp.any(mid[:, None, :top, :] == ids[None, :, None, None], axis=2)
        rank = dot32("zet,tv->zev", hit.astype(BF), before(tok_rows))
        slots = jnp.arange(SLOT, dtype=F32)
        pick = (hit[:, :, None, :] & (rank[:, :, None, :] == slots[None, None, :, None])).astype(BF)

        def route_rows(rows):
            got = dot32("zert,ztf->ezrf", pick, rows).astype(BF)
            got = got.reshape(NY * NX, NZ * SLOT, quarter)
            return lax.all_to_all(got, ("y", "x"), split_axis=0, concat_axis=0, tiled=True)

        x_own = route_rows(xz)
        d_own = route_rows(dz)
        x_sib = lax.ppermute(x_own, "c", sib)
        d_sib = lax.ppermute(d_own, "c", sib)

    with jax.named_scope("slot_weight"):
        mine = (4 * (iy * NZ + iz) + ix).astype(BF)
        on = table[:, :, :, :top, :] == mine
        p_of = jnp.sum(jnp.where(on, table[:, :, :, top:, :], jnp.zeros((), BF)).astype(F32), axis=3)
        hit_e = jnp.any(on, axis=3)
        rank_e = dot32("yzct,tv->yzcv", hit_e.astype(BF), before(tok_rows))
        pick_e = hit_e[..., None, :] & (rank_e[..., None, :] == slots[:, None])
        weight = jnp.sum(jnp.where(pick_e, p_of[..., None, :], 0.0), axis=-1)
        weight = weight.transpose(2, 0, 1, 3)
        weight = jnp.where(ic == 0, weight, weight[::-1]).reshape(-1)

    def rows_of(own, sibling):
        both = jnp.stack([own, sibling]).reshape(NC, NY, NX, NZ * SLOT, quarter)
        return both.transpose(0, 1, 3, 2, 4).reshape(NC * NY * NZ * SLOT, NX * quarter)

    with jax.named_scope("expert"):
        xin = rows_of(x_own, x_sib)
        dout = rows_of(d_own, d_sib)
        gate = dot32("rd,fd->rf", xin, wg)
        upval = dot32("rd,fd->rf", xin, wu)
        raw = dot32("rd,fd->rf", dout, wd)
        sig = jax.nn.sigmoid(gate)
        act = gate * sig
        hidden = (act * upval).astype(BF)
        score = jnp.sum(hidden.astype(F32) * raw, axis=1)
        scaled = (weight[:, None] * dout.astype(F32)).astype(BF)
        dact = weight[:, None] * raw
        dgate = (dact * upval * sig * (1.0 + gate * (1.0 - sig))).astype(BF)
        dup = (dact * act).astype(BF)
        part = dot32("rf,fd->rd", dgate, wg) + dot32("rf,fd->rd", dup, wu)
        part = part.reshape(NC, NY, NZ * SLOT, NX, quarter).transpose(0, 1, 3, 2, 4)
        part = part.reshape(NC, NY * NX, NZ * SLOT, quarter)
        sent = lax.ppermute(part[1].astype(BF), "c", sib)
        grads = jnp.stack(
            [
                dot32("rf,rd->fd", dgate, xin).astype(BF),
                dot32("rf,rd->fd", dup, xin).astype(BF),
                dot32("rf,rd->fd", hidden, scaled).astype(BF),
            ]
        )

    with jax.named_scope("weights_back"):
        half = w_gate.shape[1]
        back = []
        for m in range(2):
            inverse = [(b, a) for a, b in weight_pairs(m)]
            back.append(lax.ppermute(grads[:, m * half : (m + 1) * half], ("c", "x"), inverse))
        even = ix % 2 == 0
        first = jnp.where(even, back[0], back[1])
        second = jnp.where(even, back[1], back[0])
        grad_gate, grad_up, grad_down = (jnp.stack([first[i], second[i]]) for i in range(3))

    with jax.named_scope("score_back"):
        score = jnp.where(ic == 0, score.reshape(NC, -1), score.reshape(NC, -1)[::-1])
        scores = lax.all_gather(score, ("y", "z", "x", "c"), axis=0, tiled=False)
        scores = scores.reshape(NY * NZ * NX, NC, NC, NY, NZ, SLOT)
        scores = scores[:, 0] + scores[:, 1]
        scores = lax.dynamic_index_in_dim(scores, ic, 1, keepdims=False)
        scores = lax.dynamic_index_in_dim(scores, iy, 1, keepdims=False)
        scores = lax.dynamic_index_in_dim(scores, iz, 1, keepdims=False)
        named = route.T[:, None, :] == jnp.arange(NY * NZ * NX, dtype=jnp.int32)[None, :, None]
        hit_s = jnp.any(named, axis=0)
        rank_s = dot32("et,tv->ev", hit_s.astype(BF), before(tok_rows))
        pick_s = hit_s[:, None, :] & (rank_s[:, None, :] == slots[None, :, None])
        of_pair = jnp.sum(jnp.where(pick_s, scores[:, :, None], 0.0), axis=1)
        grad_prob = jnp.sum(jnp.where(named, of_pair[None], 0.0), axis=1).T

    with jax.named_scope("tokens_back"):
        total = (part[0] + sent.astype(F32)).astype(BF)
        home = lax.all_to_all(total, ("y", "x"), split_axis=0, concat_axis=0, tiled=True)
        home = home.reshape(NY * NX, NZ, SLOT, quarter)
        summed = dot32("zert,ezrf->ztf", pick, home).astype(BF)
        grad_tokens = lax.psum_scatter(summed, "z", scatter_dimension=0, tiled=True)[0]
    return (grad_tokens, grad_prob, grad_gate, grad_up, grad_down)


def solution(mesh):
    grid = Mesh(mesh.devices.reshape(NY, NZ, NC, NX), ("y", "z", "c", "x"))
    expert = ("y", "z", "c")
    in_specs = (
        P(expert, "x"),
        P(expert, "x"),
        P(expert, None),
        P(expert, None),
        P(expert, "x", None),
        P(expert, "x", None),
        P(expert, "x", None),
    )
    out_specs = (
        P(expert, "x"),
        P(expert, None),
        P(expert, "x", None),
        P(expert, "x", None),
        P(expert, "x", None),
    )
    return jax.shard_map(per_device, mesh=grid, in_specs=in_specs, out_specs=out_specs, check_vma=False)
```

```python
import jax
import jax.numpy as jnp
from jax import lax
from jax.experimental import pallas as pl
from jax.experimental.pallas import tpu as pltpu
from jax.sharding import Mesh, PartitionSpec as P

BF = jnp.bfloat16
F32 = jnp.float32
NY, NZ, NC, NX = 4, 8, 2, 4
SLOT = 16
TOK = 128
TOP = 8
ROWS = NZ * SLOT
FULL = ROWS + 16
Q = 512
D = NX * Q
FQ = 192
FH = 2 * FQ
DEST = NY * NX
VMEM = pl.BlockSpec(memory_space=pltpu.VMEM)
SMEM = pl.BlockSpec(memory_space=pltpu.SMEM)


def params():
    return pltpu.CompilerParams(vmem_limit_bytes=56 * 1024 * 1024)


def dot(a, b, ca, cb):
    return lax.dot_general(a, b, (((ca,), (cb,)), ((), ())), preferred_element_type=F32)


def iota(shape, axis):
    return lax.broadcasted_iota(jnp.int32, shape, axis)


def expert_of(slot_row, iz, per):
    e = slot_row // per
    return (4 * ((e // NX) * NZ + iz) + e % NX).astype(F32)


def weight_pairs(m):
    pairs = []
    for c in range(NC):
        for h in range(NX):
            k = (h + m) % 2
            pairs.append((c * NX + h, (h // 2) * NX + 2 * c + k))
    return pairs


def select_x(at_ref, g_ref, out_ref, pick_ref):
    iz = at_ref[1]
    before = (iota((TOK, TOK), 0) < iota((TOK, TOK), 1)).astype(BF)
    ids = expert_of(iota((DEST, TOK), 0), iz, 1)
    slot = (iota((DEST * SLOT, TOK), 0) % SLOT).astype(F32)
    lane = iota((DEST * SLOT, TOK), 1)
    carried = jnp.zeros((DEST * SLOT, TOK), F32)
    for z in range(NZ):
        table = g_ref[z, 2 * TOK : 2 * TOK + 2 * TOP, :TOK].astype(F32)
        hit = jnp.zeros((DEST, TOK), F32)
        chance = jnp.zeros((DEST, TOK), F32)
        for k in range(TOP):
            on = table[k : k + 1, :] == ids
            hit = jnp.where(on, 1.0, hit)
            chance = jnp.where(on, table[TOP + k : TOP + k + 1, :], chance)
        rank = dot(hit.astype(BF), before, 1, 0)
        rank = jnp.where(hit > 0.5, rank, -1.0)
        wide = jnp.broadcast_to(rank[:, None, :], (DEST, SLOT, TOK)).reshape(DEST * SLOT, TOK)
        mine = wide == slot
        chance = jnp.broadcast_to(chance[:, None, :], (DEST, SLOT, TOK)).reshape(DEST * SLOT, TOK)
        share = jnp.sum(jnp.where(mine, chance, 0.0), axis=1, keepdims=True)
        carried = jnp.where(lane == z, share, carried)
        pick = jnp.where(mine, 1.0, 0.0).astype(BF)
        pick_ref[z] = pick
        got = dot(pick, g_ref[z, :TOK, :], 1, 0).astype(BF)
        out_ref[:, z * SLOT : (z + 1) * SLOT, :] = got.reshape(DEST, SLOT, Q)
    out_ref[:, ROWS:, :TOK] = carried.astype(BF).reshape(DEST, 16, TOK)
    out_ref[:, ROWS:, TOK:] = jnp.zeros((DEST, 16, Q - TOK), BF)


def select_d(g_ref, pick_ref, out_ref):
    for z in range(NZ):
        got = dot(pick_ref[z], g_ref[z, TOK : 2 * TOK, :], 1, 0).astype(BF)
        out_ref[:, z * SLOT : (z + 1) * SLOT, :] = got.reshape(DEST, SLOT, Q)


def expert(at_ref, x_ref, d_ref, wa_ref, wb_ref, part_ref, keep_ref):
    rows = NY * ROWS

    def take(ref, h):
        return jnp.concatenate([ref[y * NX + h, :ROWS, :] for y in range(NY)], axis=0)

    def project(ref, i):
        halves = []
        for w in (wa_ref, wb_ref):
            total = jnp.zeros((rows, FQ), F32)
            for h in range(NX):
                total = total + dot(take(ref, h), w[i, :, h * Q : (h + 1) * Q], 1, 1)
            halves.append(total)
        return halves

    columns = []
    for y in range(NY):
        carried = x_ref[y * NX, ROWS:, :TOK].astype(F32)
        columns += [carried[:, z : z + 1] for z in range(NZ)]
    weight = jnp.concatenate(columns, axis=0)
    gates = project(x_ref, 0)
    ups = project(x_ref, 1)
    raws = project(d_ref, 2)
    score = jnp.zeros((rows, 1), F32)
    dgates, dups = [], []
    for m in range(2):
        gate, up, raw = gates[m], ups[m], raws[m]
        sig = 1.0 / (1.0 + jnp.exp(-gate))
        act = gate * sig
        hidden = act * up
        score = score + jnp.sum(hidden * raw, axis=1, keepdims=True)
        dact = weight * raw
        dgate = (dact * up * sig * (1.0 + gate * (1.0 - sig))).astype(BF)
        dup = (dact * act).astype(BF)
        keep_ref[m, 0] = dgate
        keep_ref[m, 1] = dup
        keep_ref[m, 2] = (weight * hidden).astype(BF)
        dgates.append(dgate)
        dups.append(dup)
    for h in range(NX):
        cols = slice(h * Q, (h + 1) * Q)
        total = dot(dgates[0], wa_ref[0, :, cols], 1, 0) + dot(dups[0], wa_ref[1, :, cols], 1, 0)
        total = total + dot(dgates[1], wb_ref[0, :, cols], 1, 0) + dot(dups[1], wb_ref[1, :, cols], 1, 0)
        for y in range(NY):
            part_ref[y * NX + h, :ROWS, :] = total[y * ROWS : (y + 1) * ROWS].astype(BF)
    lane = iota((SLOT, TOK), 1) - 2 * NZ * at_ref[2]
    coarse = score.astype(BF).astype(F32)
    fine = score - coarse
    for y in range(NY):
        block = jnp.zeros((SLOT, TOK), F32)
        for z in range(NZ):
            at = (y * NZ + z) * SLOT
            block = jnp.where(lane == z, coarse[at : at + SLOT], block)
            block = jnp.where(lane == NZ + z, fine[at : at + SLOT], block)
        for h in range(NX):
            part_ref[y * NX + h, ROWS:, :TOK] = block.astype(BF)
            part_ref[y * NX + h, ROWS:, TOK:] = jnp.zeros((SLOT, Q - TOK), BF)


def weight_grads(xo_ref, xs_ref, do_ref, ds_ref, ko_ref, ks_ref, a_ref, b_ref, flip):
    @pl.when(pl.program_id(0) == 0)
    def _():
        for i in range(3):
            for m in range(2):
                flip[i, m, :, : NY * ROWS] = ko_ref[m, i].T
                flip[i, m, :, NY * ROWS :] = ks_ref[m, i].T

    def take(own, sibling):
        pieces = [own[y, 0, :ROWS, :] for y in range(NY)] + [sibling[y, 0, :ROWS, :] for y in range(NY)]
        return jnp.concatenate(pieces, axis=0)

    x = take(xo_ref, xs_ref)
    d = take(do_ref, ds_ref)
    for i, rows in ((0, x), (1, x), (2, d)):
        a_ref[i] = dot(flip[i, 0], rows, 1, 0).astype(BF)
        b_ref[i] = dot(flip[i, 1], rows, 1, 0).astype(BF)


def combine(at_ref, g_ref, pick_ref, home_ref, out_ref):
    iz = at_ref[1]
    ids = expert_of(iota((DEST, TOK), 0), iz, 1)
    carried = home_ref[:, ROWS:, :TOK].astype(F32).reshape(DEST * SLOT, TOK)
    for z in range(NZ):
        pick = pick_ref[z]
        rows = home_ref[:, z * SLOT : (z + 1) * SLOT, :].reshape(DEST * SLOT, Q)
        out_ref[z, :TOK, :] = dot(pick, rows, 0, 0).astype(BF)
        score = carried[:, z : z + 1] + carried[:, NZ + z : NZ + z + 1]
        score = score + (carried[:, 2 * NZ + z : 2 * NZ + z + 1] + carried[:, 3 * NZ + z : 3 * NZ + z + 1])
        spread = (pick.astype(F32) * score).reshape(DEST, SLOT, TOK)
        spread = jnp.sum(spread, axis=1)
        table = g_ref[z, 2 * TOK : 2 * TOK + TOP, :TOK].astype(F32)
        lines = [
            jnp.sum(jnp.where(table[k : k + 1, :] == ids, spread, 0.0), axis=0, keepdims=True)
            for k in range(TOP)
        ]
        lines = jnp.concatenate(lines + [jnp.zeros((16 - TOP, TOK), F32)], axis=0)
        coarse = lines.astype(BF)
        out_ref[z, TOK:, :TOK] = coarse
        out_ref[z, TOK:, TOK : 2 * TOK] = (lines - coarse.astype(F32)).astype(BF)
        out_ref[z, TOK:, 2 * TOK :] = jnp.zeros((16, Q - 2 * TOK), BF)


def per_device(tokens, cotangent, route, prob, w_gate, w_up, w_down):
    iy, iz, ic, ix = (lax.axis_index(a) for a in ("y", "z", "c", "x"))
    at = jnp.stack([iy, iz, ic, ix]).astype(jnp.int32)
    sib = [(0, 1), (1, 0)]
    shape = jax.ShapeDtypeStruct

    with jax.named_scope("gather_z"):
        table = jnp.concatenate([route.T.astype(BF), prob.T], axis=0)
        table = jnp.pad(table, ((0, 0), (0, Q - TOK)))
        packed = jnp.concatenate([tokens, cotangent, table], axis=0)
        every = lax.all_gather(packed, "z", axis=0, tiled=False)

    with jax.named_scope("weights_out"):
        weights = []
        for m in range(2):
            k = (ix + m) % 2
            piece = jnp.stack([lax.dynamic_index_in_dim(w, k, 0, keepdims=False) for w in (w_gate, w_up, w_down)])
            weights.append(lax.ppermute(piece, ("c", "x"), weight_pairs(m)))
        wa, wb = weights

    with jax.named_scope("select"):
        every, wa = lax.optimization_barrier((every, wa))
        xs, pick = pl.pallas_call(
            select_x,
            out_shape=(shape((DEST, FULL, Q), BF), shape((NZ, DEST * SLOT, TOK), BF)),
            in_specs=[SMEM, VMEM],
            out_specs=(VMEM, VMEM),
            compiler_params=params(),
            name="select_x",
        )(at, every)
        x_own = lax.all_to_all(xs, ("y", "x"), split_axis=0, concat_axis=0, tiled=True)
        pick_d, wb = lax.optimization_barrier((pick, wb))
        ds = pl.pallas_call(
            select_d,
            out_shape=shape((DEST, ROWS, Q), BF),
            in_specs=[VMEM, VMEM],
            out_specs=VMEM,
            compiler_params=params(),
            name="select_d",
        )(every, pick_d)
        d_own = lax.all_to_all(ds, ("y", "x"), split_axis=0, concat_axis=0, tiled=True)
        x_sib = lax.ppermute(x_own, "c", sib)
        d_sib = lax.ppermute(d_own, "c", sib)

    run = pl.pallas_call(
        expert,
        out_shape=(shape((DEST, FULL, Q), BF), shape((2, 3, NY * ROWS, FQ), BF)),
        in_specs=[SMEM, VMEM, VMEM, VMEM, VMEM],
        out_specs=(VMEM, VMEM),
        compiler_params=params(),
        name="expert",
    )
    with jax.named_scope("expert"):
        part_own, keep_own = run(at, x_own, d_own, wa, wb)
        part_sib, keep_sib = run(at, x_sib, d_sib, wa, wb)
        sent = lax.ppermute(part_sib, "c", sib)

    with jax.named_scope("weights_back"):
        x_spec = pl.BlockSpec((NY, 1, FULL, Q), lambda h: (0, h, 0, 0))
        d_spec = pl.BlockSpec((NY, 1, ROWS, Q), lambda h: (0, h, 0, 0))
        k_spec = pl.BlockSpec((2, 3, NY * ROWS, FQ), lambda h: (0, 0, 0, 0))
        o_spec = pl.BlockSpec((3, FQ, Q), lambda h: (0, 0, h))
        ga, gb = pl.pallas_call(
            weight_grads,
            grid=(NX,),
            out_shape=(shape((3, FQ, D), BF),) * 2,
            in_specs=[x_spec, x_spec, d_spec, d_spec, k_spec, k_spec],
            out_specs=(o_spec, o_spec),
            scratch_shapes=[pltpu.VMEM((3, 2, FQ, 2 * NY * ROWS), BF)],
            compiler_params=params(),
            name="weight_grads",
        )(
            x_own.reshape(NY, NX, FULL, Q),
            x_sib.reshape(NY, NX, FULL, Q),
            d_own.reshape(NY, NX, ROWS, Q),
            d_sib.reshape(NY, NX, ROWS, Q),
            keep_own,
            keep_sib,
        )
        back = []
        for m, g in ((0, ga), (1, gb)):
            inverse = [(b, a) for a, b in weight_pairs(m)]
            back.append(lax.ppermute(g, ("c", "x"), inverse))
        even = ix % 2 == 0
        first = jnp.where(even, back[0], back[1])
        second = jnp.where(even, back[1], back[0])
        grad_gate, grad_up, grad_down = (jnp.stack([first[i], second[i]]) for i in range(3))

    with jax.named_scope("tokens_back"):
        total = (part_own.astype(F32) + sent.astype(F32)).astype(BF)
        home = lax.all_to_all(total, ("y", "x"), split_axis=0, concat_axis=0, tiled=True)
        partial = pl.pallas_call(
            combine,
            out_shape=shape((NZ, TOK + 16, Q), BF),
            in_specs=[SMEM, VMEM, VMEM, VMEM],
            out_specs=VMEM,
            compiler_params=params(),
            name="combine",
        )(at, every, pick, home)
        last = lax.all_to_all(partial, "z", split_axis=0, concat_axis=0, tiled=True).astype(F32)
        grad_tokens = jnp.sum(last[:, :TOK], axis=0).astype(BF)
        lines = jnp.sum(last[:, TOK : TOK + TOP, : 2 * TOK], axis=0)
        grad_prob = (lines[:, :TOK] + lines[:, TOK:]).T
    return (grad_tokens, grad_prob, grad_gate, grad_up, grad_down)


def solution(mesh):
    grid = Mesh(mesh.devices.reshape(NY, NZ, NC, NX), ("y", "z", "c", "x"))
    owner = ("y", "z", "c")
    wide = P(owner, "x")
    thin = P(owner, None)
    deep = P(owner, "x", None)
    return jax.shard_map(
        per_device,
        mesh=grid,
        in_specs=(wide, wide, thin, thin, deep, deep, deep),
        out_specs=(wide, thin, deep, deep, deep),
        check_vma=False,
    )
```

```python
import jax
import jax.numpy as jnp
from jax import lax
from jax.experimental import pallas as pl
from jax.experimental.pallas import tpu as pltpu
from jax.sharding import Mesh, PartitionSpec as P

BF = jnp.bfloat16
F32 = jnp.float32
NY, NZ, NC, NX = 4, 8, 2, 4
SLOT = 16
TOK = 128
TOP = 8
ROWS = NZ * SLOT
FULL = ROWS + 16
Q = 512
D = NX * Q
FQ = 192
FH = 2 * FQ
DEST = NY * NX
VMEM = pl.BlockSpec(memory_space=pltpu.VMEM)
SMEM = pl.BlockSpec(memory_space=pltpu.SMEM)


def params(mib=32):
    return pltpu.CompilerParams(vmem_limit_bytes=mib * 1024 * 1024)


def dot(a, b, ca, cb):
    return lax.dot_general(a, b, (((ca,), (cb,)), ((), ())), preferred_element_type=F32)


def iota(shape, axis):
    return lax.broadcasted_iota(jnp.int32, shape, axis)


def expert_of(slot_row, iz, per):
    e = slot_row // per
    return (4 * ((e // NX) * NZ + iz) + e % NX).astype(F32)


def weight_pairs(m):
    pairs = []
    for c in range(NC):
        for h in range(NX):
            k = (h + m) % 2
            pairs.append((c * NX + h, (h // 2) * NX + 2 * c + k))
    return pairs


def select_x(at_ref, g_ref, out_ref, pick_ref):
    iz = at_ref[1]
    before = (iota((TOK, TOK), 0) < iota((TOK, TOK), 1)).astype(BF)
    ids = expert_of(iota((DEST, TOK), 0), iz, 1)
    slot = (iota((DEST * SLOT, TOK), 0) % SLOT).astype(F32)
    lane = iota((DEST * SLOT, TOK), 1)
    carried = jnp.zeros((DEST * SLOT, TOK), F32)
    for z in range(NZ):
        table = g_ref[z, 2 * TOK : 2 * TOK + 2 * TOP, :TOK].astype(F32)
        hit = jnp.zeros((DEST, TOK), F32)
        chance = jnp.zeros((DEST, TOK), F32)
        for k in range(TOP):
            on = table[k : k + 1, :] == ids
            hit = jnp.where(on, 1.0, hit)
            chance = jnp.where(on, table[TOP + k : TOP + k + 1, :], chance)
        rank = dot(hit.astype(BF), before, 1, 0)
        rank = jnp.where(hit > 0.5, rank, -1.0)
        wide = jnp.broadcast_to(rank[:, None, :], (DEST, SLOT, TOK)).reshape(DEST * SLOT, TOK)
        mine = wide == slot
        chance = jnp.broadcast_to(chance[:, None, :], (DEST, SLOT, TOK)).reshape(DEST * SLOT, TOK)
        share = jnp.sum(jnp.where(mine, chance, 0.0), axis=1, keepdims=True)
        carried = jnp.where(lane == z, share, carried)
        pick = jnp.where(mine, 1.0, 0.0).astype(BF)
        pick_ref[z] = pick
        got = dot(pick, g_ref[z, :TOK, :], 1, 0).astype(BF)
        out_ref[:, z * SLOT : (z + 1) * SLOT, :] = got.reshape(DEST, SLOT, Q)
    out_ref[:, ROWS:, :TOK] = carried.astype(BF).reshape(DEST, 16, TOK)
    out_ref[:, ROWS:, TOK:] = jnp.zeros((DEST, 16, Q - TOK), BF)


def select_d(g_ref, pick_ref, out_ref):
    for z in range(NZ):
        got = dot(pick_ref[z], g_ref[z, TOK : 2 * TOK, :], 1, 0).astype(BF)
        out_ref[:, z * SLOT : (z + 1) * SLOT, :] = got.reshape(DEST, SLOT, Q)


def take(ref, h):
    return jnp.concatenate([ref[y * NX + h, :ROWS, :] for y in range(NY)], axis=0)


def both(w, i, h):
    cols = slice(h * Q, (h + 1) * Q)
    second = w[1][0, :, cols] if i == 0 else w[2][i - 1, :, cols]
    return jnp.concatenate([w[0][i, :, cols], second], axis=0)


def project(ref, w, i):
    total = dot(take(ref, 0), both(w, i, 0), 1, 1)
    for h in range(1, NX):
        total = total + dot(take(ref, h), both(w, i, h), 1, 1)
    return total


def gates(x_ref, wa_ref, wb_ref, wc_ref, pre_ref, keep_ref):
    w = (wa_ref, wb_ref, wc_ref)
    columns = []
    for y in range(NY):
        carried = x_ref[y * NX, ROWS:, :TOK].astype(F32)
        columns += [carried[:, z : z + 1] for z in range(NZ)]
    weight = jnp.concatenate(columns, axis=0)
    gate = project(x_ref, w, 0)
    up = project(x_ref, w, 1)
    sig = 1.0 / (1.0 + jnp.exp(-gate))
    act = gate * sig
    hidden = act * up
    pre_ref[0] = hidden
    pre_ref[1] = weight * (up * (sig * (1.0 + gate * (1.0 - sig))))
    pre_ref[2] = weight * act
    keep_ref[...] = (weight * hidden).astype(BF)


def expert(at_ref, pre_ref, d_ref, wa_ref, wb_ref, wc_ref, part_ref, keep_ref):
    w = (wa_ref, wb_ref, wc_ref)
    raw = project(d_ref, w, 2)
    score = jnp.sum(pre_ref[0] * raw, axis=1, keepdims=True)
    keep_ref[0] = (raw * pre_ref[1]).astype(BF)
    keep_ref[1] = (raw * pre_ref[2]).astype(BF)
    for h in range(NX):
        total = dot(keep_ref[0], both(w, 0, h), 1, 0)
        total = total + dot(keep_ref[1], both(w, 1, h), 1, 0)
        for y in range(NY):
            part_ref[y * NX + h, :ROWS, :] = total[y * ROWS : (y + 1) * ROWS].astype(BF)
    lane = iota((SLOT, TOK), 1) - 2 * NZ * at_ref[2]
    coarse = score.astype(BF).astype(F32)
    fine = score - coarse
    for y in range(NY):
        block = jnp.zeros((SLOT, TOK), F32)
        for z in range(NZ):
            at = (y * NZ + z) * SLOT
            block = jnp.where(lane == z, coarse[at : at + SLOT], block)
            block = jnp.where(lane == NZ + z, fine[at : at + SLOT], block)
        for h in range(NX):
            part_ref[y * NX + h, ROWS:, :TOK] = block.astype(BF)
            part_ref[y * NX + h, ROWS:, TOK:] = jnp.zeros((SLOT, Q - TOK), BF)


def weight_grads(xo_ref, xs_ref, do_ref, ds_ref, ho_ref, hs_ref, ko_ref, ks_ref, a_ref, b_ref, flip):
    @pl.when(pl.program_id(0) == 0)
    def _():
        for i in range(2):
            flip[i, :, : NY * ROWS] = ko_ref[i].T
            flip[i, :, NY * ROWS :] = ks_ref[i].T
        flip[2, :, : NY * ROWS] = ho_ref[...].T
        flip[2, :, NY * ROWS :] = hs_ref[...].T

    def gather(own, sibling):
        pieces = [own[y, 0, :ROWS, :] for y in range(NY)] + [sibling[y, 0, :ROWS, :] for y in range(NY)]
        return jnp.concatenate(pieces, axis=0)

    x = gather(xo_ref, xs_ref)
    d = gather(do_ref, ds_ref)
    for i, rows in ((0, x), (1, x), (2, d)):
        grad = dot(flip[i], rows, 1, 0).astype(BF)
        a_ref[i] = grad[:FQ]
        b_ref[i] = grad[FQ:]


def place(at_ref, a_ref, b_ref, gate_ref, up_ref, down_ref, sem):
    odd = at_ref[3] % 2
    copies = []
    for m, src in ((0, a_ref), (1, b_ref)):
        k = (odd + m) % 2
        for i, dst in enumerate((gate_ref, up_ref, down_ref)):
            copies.append(pltpu.make_async_copy(src.at[i], dst.at[k], sem.at[m, i]))
    for copy in copies:
        copy.start()
    for copy in copies:
        copy.wait()


def combine(at_ref, g_ref, pick_ref, home_ref, out_ref):
    iz = at_ref[1]
    ids = expert_of(iota((DEST, TOK), 0), iz, 1)
    carried = home_ref[:, ROWS:, :TOK].astype(F32).reshape(DEST * SLOT, TOK)
    for z in range(NZ):
        pick = pick_ref[z]
        rows = home_ref[:, z * SLOT : (z + 1) * SLOT, :].reshape(DEST * SLOT, Q)
        out_ref[z, :TOK, :] = dot(pick, rows, 0, 0).astype(BF)
        score = carried[:, z : z + 1] + carried[:, NZ + z : NZ + z + 1]
        score = score + (carried[:, 2 * NZ + z : 2 * NZ + z + 1] + carried[:, 3 * NZ + z : 3 * NZ + z + 1])
        spread = (pick.astype(F32) * score).reshape(DEST, SLOT, TOK)
        spread = jnp.sum(spread, axis=1)
        table = g_ref[z, 2 * TOK : 2 * TOK + TOP, :TOK].astype(F32)
        lines = [
            jnp.sum(jnp.where(table[k : k + 1, :] == ids, spread, 0.0), axis=0, keepdims=True)
            for k in range(TOP)
        ]
        lines = jnp.concatenate(lines + [jnp.zeros((16 - TOP, TOK), F32)], axis=0)
        coarse = lines.astype(BF)
        out_ref[z, TOK:, :TOK] = coarse
        out_ref[z, TOK:, TOK : 2 * TOK] = (lines - coarse.astype(F32)).astype(BF)
        out_ref[z, TOK:, 2 * TOK :] = jnp.zeros((16, Q - 2 * TOK), BF)


def per_device(tokens, cotangent, route, prob, w_gate, w_up, w_down):
    iy, iz, ic, ix = (lax.axis_index(a) for a in ("y", "z", "c", "x"))
    at = jnp.stack([iy, iz, ic, ix]).astype(jnp.int32)
    sib = [(0, 1), (1, 0)]
    shape = jax.ShapeDtypeStruct

    with jax.named_scope("gather_z"):
        table = jnp.concatenate([route.T.astype(BF), prob.T], axis=0)
        table = jnp.pad(table, ((0, 0), (0, Q - TOK)))
        packed = jnp.concatenate([tokens, cotangent, table], axis=0)
        every = lax.all_gather(packed, "z", axis=0, tiled=False)

    with jax.named_scope("weights_out"):
        weights = []
        for m, mats in ((0, (w_gate, w_up, w_down)), (1, (w_gate,)), (1, (w_up, w_down))):
            k = (ix + m) % 2
            piece = jnp.stack([lax.dynamic_index_in_dim(w, k, 0, keepdims=False) for w in mats])
            if len(weights) == 2:
                piece, weights[0] = lax.optimization_barrier((piece, weights[0]))
            weights.append(lax.ppermute(piece, ("c", "x"), weight_pairs(m)))

    with jax.named_scope("select"):
        every, *weights[:2] = lax.optimization_barrier((every, *weights[:2]))
        xs, pick = pl.pallas_call(
            select_x,
            out_shape=(shape((DEST, FULL, Q), BF), shape((NZ, DEST * SLOT, TOK), BF)),
            in_specs=[SMEM, VMEM],
            out_specs=(VMEM, VMEM),
            compiler_params=params(),
            name="select_x",
        )(at, every)
        x_own = lax.all_to_all(xs, ("y", "x"), split_axis=0, concat_axis=0, tiled=True)
        ds = pl.pallas_call(
            select_d,
            out_shape=shape((DEST, ROWS, Q), BF),
            in_specs=[VMEM, VMEM],
            out_specs=VMEM,
            compiler_params=params(),
            name="select_d",
        )(every, pick)
        ds, weights[2] = lax.optimization_barrier((ds, weights[2]))
        d_own = lax.all_to_all(ds, ("y", "x"), split_axis=0, concat_axis=0, tiled=True)
        x_sib = lax.ppermute(x_own, "c", sib)

    half = NY * ROWS
    with jax.named_scope("gates"):
        ahead = pl.pallas_call(
            gates,
            out_shape=(shape((3, half, FH), F32), shape((half, FH), BF)),
            in_specs=[VMEM] * 4,
            out_specs=(VMEM, VMEM),
            compiler_params=params(),
            name="gates",
        )
        pre_own, hid_own = ahead(x_own, *weights)
        pre_sib, hid_sib = ahead(x_sib, *weights)
        d_own, pre_own, pre_sib = lax.optimization_barrier((d_own, pre_own, pre_sib))
        d_sib = lax.ppermute(d_own, "c", sib)
    run = pl.pallas_call(
        expert,
        out_shape=(shape((DEST, FULL, Q), BF), shape((2, half, FH), BF)),
        in_specs=[SMEM] + [VMEM] * 5,
        out_specs=(VMEM, VMEM),
        compiler_params=params(),
        name="expert",
    )
    with jax.named_scope("expert"):
        part_sib, keep_sib = run(at, pre_sib, d_sib, *weights)
        sent = lax.ppermute(part_sib, "c", sib)
        part_own, keep_own = run(at, pre_own, d_own, *weights)
        total = (part_own.astype(F32) + sent.astype(F32)).astype(BF)
        total, keep_own, keep_sib = lax.optimization_barrier((total, keep_own, keep_sib))

    with jax.named_scope("weights_back"):
        x_spec = pl.BlockSpec((NY, 1, FULL, Q), lambda h: (0, h, 0, 0))
        d_spec = pl.BlockSpec((NY, 1, ROWS, Q), lambda h: (0, h, 0, 0))
        h_spec = pl.BlockSpec((half, FH), lambda h: (0, 0))
        k_spec = pl.BlockSpec((2, half, FH), lambda h: (0, 0, 0))
        o_spec = pl.BlockSpec((3, FQ, Q), lambda h: (0, 0, h))
        ga, gb = pl.pallas_call(
            weight_grads,
            grid=(NX,),
            out_shape=(shape((3, FQ, D), BF),) * 2,
            in_specs=[x_spec, x_spec, d_spec, d_spec, h_spec, h_spec, k_spec, k_spec],
            out_specs=(o_spec, o_spec),
            scratch_shapes=[pltpu.VMEM((3, FH, 2 * half), BF)],
            compiler_params=params(),
            name="weight_grads",
        )(
            x_own.reshape(NY, NX, FULL, Q),
            x_sib.reshape(NY, NX, FULL, Q),
            d_own.reshape(NY, NX, ROWS, Q),
            d_sib.reshape(NY, NX, ROWS, Q),
            hid_own,
            hid_sib,
            keep_own,
            keep_sib,
        )
        back = []
        for m, g in ((0, ga), (1, gb)):
            inverse = [(b, a) for a, b in weight_pairs(m)]
            back.append(lax.ppermute(g, ("c", "x"), inverse))
        anywhere = pl.BlockSpec(memory_space=pl.ANY)
        grad_gate, grad_up, grad_down = pl.pallas_call(
            place,
            out_shape=(shape((2, FQ, D), BF),) * 3,
            in_specs=[SMEM, anywhere, anywhere],
            out_specs=(anywhere,) * 3,
            scratch_shapes=[pltpu.SemaphoreType.DMA((2, 3))],
            compiler_params=params(),
            name="place",
        )(at, back[0], back[1])

    with jax.named_scope("tokens_back"):
        home = lax.all_to_all(total, ("y", "x"), split_axis=0, concat_axis=0, tiled=True)
        partial = pl.pallas_call(
            combine,
            out_shape=shape((NZ, TOK + 16, Q), BF),
            in_specs=[SMEM, VMEM, VMEM, VMEM],
            out_specs=VMEM,
            compiler_params=params(),
            name="combine",
        )(at, every, pick, home)
        last = lax.all_to_all(partial, "z", split_axis=0, concat_axis=0, tiled=True).astype(F32)
        grad_tokens = jnp.sum(last[:, :TOK], axis=0).astype(BF)
        lines = jnp.sum(last[:, TOK : TOK + TOP, : 2 * TOK], axis=0)
        grad_prob = (lines[:, :TOK] + lines[:, TOK:]).T
    return (grad_tokens, grad_prob, grad_gate, grad_up, grad_down)


def solution(mesh):
    grid = Mesh(mesh.devices.reshape(NY, NZ, NC, NX), ("y", "z", "c", "x"))
    owner = ("y", "z", "c")
    wide = P(owner, "x")
    thin = P(owner, None)
    deep = P(owner, "x", None)
    return jax.shard_map(
        per_device,
        mesh=grid,
        in_specs=(wide, wide, thin, thin, deep, deep, deep),
        out_specs=(wide, thin, deep, deep, deep),
        check_vma=False,
    )
```

```python
import jax
import jax.numpy as jnp
from jax import lax
from jax.experimental import pallas as pl
from jax.experimental.pallas import tpu as pltpu
from jax.sharding import Mesh, PartitionSpec as P

BF = jnp.bfloat16
F32 = jnp.float32
NY, NZ, NC, NX = 4, 8, 2, 4
SLOT = 16
TOK = 128
TOP = 8
PEER = NY * NZ
ROWS = PEER * SLOT
Q = 512
D = NX * Q
WIDE = D + 128
FQ = 192
FH = 2 * FQ
VMEM = pl.BlockSpec(memory_space=pltpu.VMEM)
SMEM = pl.BlockSpec(memory_space=pltpu.SMEM)


def params(mib=32):
    return pltpu.CompilerParams(vmem_limit_bytes=mib * 1024 * 1024)


def dot(a, b, ca, cb):
    return lax.dot_general(a, b, (((ca,), (cb,)), ((), ())), preferred_element_type=F32)


def iota(shape, axis):
    return lax.broadcasted_iota(jnp.int32, shape, axis)


def weight_pairs(m):
    pairs = []
    for c in range(NC):
        for h in range(NX):
            k = (h + m) % 2
            pairs.append((c * NX + h, (h // 2) * NX + 2 * c + k))
    return pairs


def select_x(at_ref, table_ref, x_ref, out_ref, pick_ref):
    ids = (NX * iota((PEER, TOK), 0) + at_ref[3]).astype(F32)
    before = (iota((TOK, TOK), 0) < iota((TOK, TOK), 1)).astype(BF)
    slot = (iota((ROWS, TOK), 0) % SLOT).astype(F32)
    lane = iota((ROWS, TOK), 1)
    table = table_ref[...]
    hit = jnp.zeros((PEER, TOK), F32)
    chance = jnp.zeros((PEER, TOK), F32)
    for k in range(TOP):
        on = table[k : k + 1, :] == ids
        hit = jnp.where(on, 1.0, hit)
        chance = jnp.where(on, table[TOP + k : TOP + k + 1, :], chance)
    rank = dot(hit.astype(BF), before, 1, 0)
    rank = jnp.where(hit > 0.5, rank, -1.0)
    rank = jnp.broadcast_to(rank[:, None, :], (PEER, SLOT, TOK)).reshape(ROWS, TOK)
    chance = jnp.broadcast_to(chance[:, None, :], (PEER, SLOT, TOK)).reshape(ROWS, TOK)
    mine = rank == slot
    share = jnp.sum(jnp.where(mine, chance, 0.0), axis=1, keepdims=True)
    pick = jnp.where(mine, 1.0, 0.0).astype(BF)
    pick_ref[...] = pick
    for h in range(NX):
        out_ref[:, h * Q : (h + 1) * Q] = dot(pick, x_ref[h], 1, 0).astype(BF)
    out_ref[:, D:] = jnp.where(lane == 0, share, 0.0).astype(BF)


def select_d(pick_ref, d_ref, out_ref):
    for h in range(NX):
        out_ref[:, h * Q : (h + 1) * Q] = dot(pick_ref[...], d_ref[h], 1, 0).astype(BF)


def both(wa_ref, wb_ref, i, h):
    cols = slice(h * Q, (h + 1) * Q)
    return jnp.concatenate([wa_ref[i, :, cols], wb_ref[i, :, cols]], axis=0)


def project(ref, wa_ref, wb_ref, i):
    total = dot(ref[:, :Q], both(wa_ref, wb_ref, i, 0), 1, 1)
    for h in range(1, NX):
        total = total + dot(ref[:, h * Q : (h + 1) * Q], both(wa_ref, wb_ref, i, h), 1, 1)
    return total


def gates(x_ref, wa_ref, wb_ref, pre_ref, keep_ref):
    weight = x_ref[:, D:].astype(F32)[:, :1]
    gate = project(x_ref, wa_ref, wb_ref, 0)
    up = project(x_ref, wa_ref, wb_ref, 1)
    sig = 1.0 / (1.0 + jnp.exp(-gate))
    act = gate * sig
    hidden = act * up
    pre_ref[0] = hidden
    pre_ref[1] = weight * (up * (sig * (1.0 + gate * (1.0 - sig))))
    pre_ref[2] = weight * act
    keep_ref[...] = (weight * hidden).astype(BF)


def expert(at_ref, pre_ref, d_ref, wa_ref, wb_ref, part_ref, keep_ref):
    raw = project(d_ref, wa_ref, wb_ref, 2)
    score = jnp.sum(pre_ref[0] * raw, axis=1, keepdims=True)
    keep_ref[0] = (raw * pre_ref[1]).astype(BF)
    keep_ref[1] = (raw * pre_ref[2]).astype(BF)
    for h in range(NX):
        total = dot(keep_ref[0], both(wa_ref, wb_ref, 0, h), 1, 0)
        total = total + dot(keep_ref[1], both(wa_ref, wb_ref, 1, h), 1, 0)
        part_ref[:, h * Q : (h + 1) * Q] = total.astype(BF)
    lane = iota((ROWS, TOK), 1) - 2 * at_ref[2]
    coarse = score.astype(BF).astype(F32)
    carried = jnp.where(lane == 0, coarse, jnp.where(lane == 1, score - coarse, 0.0))
    part_ref[:, D:] = carried.astype(BF)


def weight_grads(xo_ref, xs_ref, do_ref, ds_ref, ho_ref, hs_ref, ko_ref, ks_ref, a_ref, b_ref, flip):
    @pl.when(pl.program_id(0) == 0)
    def _():
        for i in range(2):
            flip[i, :, :ROWS] = ko_ref[i].T
            flip[i, :, ROWS:] = ks_ref[i].T
        flip[2, :, :ROWS] = ho_ref[...].T
        flip[2, :, ROWS:] = hs_ref[...].T

    x = jnp.concatenate([xo_ref[...], xs_ref[...]], axis=0)
    d = jnp.concatenate([do_ref[...], ds_ref[...]], axis=0)
    for i, rows in ((0, x), (1, x), (2, d)):
        grad = dot(flip[i], rows, 1, 0).astype(BF)
        a_ref[i] = grad[:FQ]
        b_ref[i] = grad[FQ:]


def place(at_ref, a_ref, b_ref, gate_ref, up_ref, down_ref):
    odd = at_ref[3] % 2
    for i, out in enumerate((gate_ref, up_ref, down_ref)):
        out[odd] = a_ref[i]
        out[1 - odd] = b_ref[i]


def combine(at_ref, table_ref, pick_ref, home_ref, out_ref):
    ids = (NX * iota((PEER, TOK), 0) + at_ref[3]).astype(F32)
    pick = pick_ref[...]
    carried = home_ref[:, D:].astype(F32)
    score = (carried[:, 0:1] + carried[:, 1:2]) + (carried[:, 2:3] + carried[:, 3:4])
    spread = jnp.sum((pick.astype(F32) * score).reshape(PEER, SLOT, TOK), axis=1)
    table = table_ref[...]
    lines = [
        jnp.sum(jnp.where(table[k : k + 1, :] == ids, spread, 0.0), axis=0, keepdims=True) for k in range(TOP)
    ]
    lines = jnp.concatenate(lines + [jnp.zeros((16 - TOP, TOK), F32)], axis=0)
    coarse = lines.astype(BF)
    fine = (lines - coarse.astype(F32)).astype(BF)
    for h in range(NX):
        out_ref[h, :TOK, :] = dot(pick, home_ref[:, h * Q : (h + 1) * Q], 0, 0).astype(BF)
        out_ref[h, TOK:, :TOK] = coarse
        out_ref[h, TOK:, TOK : 2 * TOK] = fine
        out_ref[h, TOK:, 2 * TOK :] = jnp.zeros((16, Q - 2 * TOK), BF)


def per_device(tokens, cotangent, route, prob, w_gate, w_up, w_down):
    at = jnp.stack([lax.axis_index(a) for a in ("y", "z", "c", "x")]).astype(jnp.int32)
    ix = lax.axis_index("x")
    sib = [(0, 1), (1, 0)]
    shape = jax.ShapeDtypeStruct

    def to_experts(rows):
        rows = rows.reshape(PEER, SLOT, rows.shape[1])
        rows = lax.all_to_all(rows, ("y", "z"), split_axis=0, concat_axis=0, tiled=True)
        return rows.reshape(ROWS, rows.shape[2])

    with jax.named_scope("select_x"):
        xg = lax.all_gather(tokens, "x", axis=0, tiled=False)
        table = jnp.concatenate([route.T.astype(F32), prob.T.astype(F32)], axis=0)
        xs, pick = pl.pallas_call(
            select_x,
            out_shape=(shape((ROWS, WIDE), BF), shape((ROWS, TOK), BF)),
            in_specs=[SMEM, VMEM, VMEM],
            out_specs=(VMEM, VMEM),
            compiler_params=params(),
            name="select_x",
        )(at, table, xg)
        x_own = to_experts(xs)

    with jax.named_scope("select_d"):
        pick, cotangent = lax.optimization_barrier((pick, cotangent))
        dg = lax.all_gather(cotangent, "x", axis=0, tiled=False)
        ds = pl.pallas_call(
            select_d,
            out_shape=shape((ROWS, D), BF),
            in_specs=[VMEM, VMEM],
            out_specs=VMEM,
            compiler_params=params(),
            name="select_d",
        )(pick, dg)

    with jax.named_scope("weights_out"):
        pick, *mats = lax.optimization_barrier((pick, w_gate, w_up, w_down))
        weights = []
        for m in range(2):
            k = (ix + m) % 2
            piece = jnp.stack([lax.dynamic_index_in_dim(w, k, 0, keepdims=False) for w in mats])
            weights.append(lax.ppermute(piece, ("c", "x"), weight_pairs(m)))

    with jax.named_scope("gates"):
        x_own, ds, *weights = lax.optimization_barrier((x_own, ds, *weights))
        d_own = to_experts(ds)
        x_sib = lax.ppermute(x_own, "c", sib)
        ahead = pl.pallas_call(
            gates,
            out_shape=(shape((3, ROWS, FH), F32), shape((ROWS, FH), BF)),
            in_specs=[VMEM] * 3,
            out_specs=(VMEM, VMEM),
            compiler_params=params(),
            name="gates",
        )
        pre_own, hid_own = ahead(x_own, *weights)
        pre_sib, hid_sib = ahead(x_sib, *weights)
        d_own, pre_own, pre_sib = lax.optimization_barrier((d_own, pre_own, pre_sib))

    with jax.named_scope("expert"):
        d_sib = lax.ppermute(d_own, "c", sib)
        run = pl.pallas_call(
            expert,
            out_shape=(shape((ROWS, WIDE), BF), shape((2, ROWS, FH), BF)),
            in_specs=[SMEM] + [VMEM] * 4,
            out_specs=(VMEM, VMEM),
            compiler_params=params(),
            name="expert",
        )
        part_sib, keep_sib = run(at, pre_sib, d_sib, *weights)
        sent = lax.ppermute(part_sib, "c", sib)
        part_own, keep_own = run(at, pre_own, d_own, *weights)
        total = (part_own.astype(F32) + sent.astype(F32)).astype(BF)
        total, keep_own, keep_sib = lax.optimization_barrier((total, keep_own, keep_sib))

    with jax.named_scope("weights_back"):
        cut = pl.BlockSpec((ROWS, Q), lambda h: (0, h))
        h_spec = pl.BlockSpec((ROWS, FH), lambda h: (0, 0))
        k_spec = pl.BlockSpec((2, ROWS, FH), lambda h: (0, 0, 0))
        o_spec = pl.BlockSpec((3, FQ, Q), lambda h: (0, 0, h))
        pieces = pl.pallas_call(
            weight_grads,
            grid=(NX,),
            out_shape=(shape((3, FQ, D), BF),) * 2,
            in_specs=[cut] * 4 + [h_spec, h_spec, k_spec, k_spec],
            out_specs=(o_spec, o_spec),
            scratch_shapes=[pltpu.VMEM((3, FH, 2 * ROWS), BF)],
            compiler_params=params(),
            name="weight_grads",
        )(x_own, x_sib, d_own, d_sib, hid_own, hid_sib, keep_own, keep_sib)
        back = []
        for m, g in enumerate(pieces):
            inverse = [(b, a) for a, b in weight_pairs(m)]
            back.append(lax.ppermute(g, ("c", "x"), inverse))
        part_rows = FQ // 4
        grad_gate, grad_up, grad_down = pl.pallas_call(
            place,
            grid=(4,),
            out_shape=(shape((2, FQ, D), BF),) * 3,
            in_specs=[SMEM] + [pl.BlockSpec((3, part_rows, D), lambda i: (0, i, 0))] * 2,
            out_specs=(pl.BlockSpec((2, part_rows, D), lambda i: (0, i, 0)),) * 3,
            compiler_params=params(),
            name="place",
        )(at, *back)

    with jax.named_scope("tokens_back"):
        home = to_experts(total)
        partial = pl.pallas_call(
            combine,
            out_shape=shape((NX, TOK + 16, Q), BF),
            in_specs=[SMEM, VMEM, VMEM, VMEM],
            out_specs=VMEM,
            compiler_params=params(),
            name="combine",
        )(at, table, pick, home)
        last = lax.all_to_all(partial, "x", split_axis=0, concat_axis=0, tiled=True).astype(F32)
        grad_tokens = jnp.sum(last[:, :TOK], axis=0).astype(BF)
        lines = jnp.sum(last[:, TOK : TOK + TOP, : 2 * TOK], axis=0)
        grad_prob = (lines[:, :TOK] + lines[:, TOK:]).T
    return (grad_tokens, grad_prob, grad_gate, grad_up, grad_down)


def solution(mesh):
    grid = Mesh(mesh.devices.reshape(NY, NZ, NC, NX), ("y", "z", "c", "x"))
    owner = ("y", "z", "c")
    wide = P(owner, "x")
    thin = P(owner, None)
    deep = P(owner, "x", None)
    return jax.shard_map(
        per_device,
        mesh=grid,
        in_specs=(wide, wide, thin, thin, deep, deep, deep),
        out_specs=(wide, thin, deep, deep, deep),
        check_vma=False,
    )
```

```python
import jax
import jax.numpy as jnp
from jax import lax
from jax.experimental import pallas as pl
from jax.experimental.pallas import tpu as pltpu
from jax.sharding import Mesh, PartitionSpec as P

BF = jnp.bfloat16
F32 = jnp.float32
NY, NZ, NC, NX = 4, 8, 2, 4
SLOT = 16
TOK = 128
TOP = 8
PEER = NY * NZ
ROWS = PEER * SLOT
Q = 512
D = NX * Q
DEST = NY * NX
PIECE = NZ * SLOT
WIDE = D + 128
FQ = 192
FH = 2 * FQ
VMEM = pl.BlockSpec(memory_space=pltpu.VMEM)
SMEM = pl.BlockSpec(memory_space=pltpu.SMEM)


def params(mib=20):
    return pltpu.CompilerParams(vmem_limit_bytes=mib * 1024 * 1024)


def dot(a, b, ca, cb):
    return lax.dot_general(a, b, (((ca,), (cb,)), ((), ())), preferred_element_type=F32)


def iota(shape, axis):
    return lax.broadcasted_iota(jnp.int32, shape, axis)


def weight_pairs(m):
    pairs = []
    for c in range(NC):
        for h in range(NX):
            k = (h + m) % 2
            pairs.append((c * NX + h, (h // 2) * NX + 2 * c + k))
    return pairs


def select_x(at_ref, table_ref, x_ref, out_ref, pick_ref):
    ids = (NX * iota((PEER, TOK), 0) + at_ref[3]).astype(F32)
    before = (iota((TOK, TOK), 0) < iota((TOK, TOK), 1)).astype(BF)
    slot = (iota((ROWS, TOK), 0) % SLOT).astype(F32)
    lane = iota((ROWS, TOK), 1)
    table = table_ref[...]
    hit = jnp.zeros((PEER, TOK), F32)
    chance = jnp.zeros((PEER, TOK), F32)
    for k in range(TOP):
        on = table[k : k + 1, :] == ids
        hit = jnp.where(on, 1.0, hit)
        chance = jnp.where(on, table[TOP + k : TOP + k + 1, :], chance)
    rank = dot(hit.astype(BF), before, 1, 0)
    rank = jnp.where(hit > 0.5, rank, -1.0)
    rank = jnp.broadcast_to(rank[:, None, :], (PEER, SLOT, TOK)).reshape(ROWS, TOK)
    chance = jnp.broadcast_to(chance[:, None, :], (PEER, SLOT, TOK)).reshape(ROWS, TOK)
    mine = rank == slot
    share = jnp.sum(jnp.where(mine, chance, 0.0), axis=1, keepdims=True)
    pick = jnp.where(mine, 1.0, 0.0).astype(BF)
    pick_ref[...] = pick
    for h in range(NX):
        out_ref[:, h * Q : (h + 1) * Q] = dot(pick, x_ref[h], 1, 0).astype(BF)
    out_ref[:, D:] = jnp.where(lane == 0, share, 0.0).astype(BF)


def select_d(at_ref, g_ref, out_ref):
    e = iota((DEST, TOK), 0)
    ids = (NX * ((e // NX) * NZ + at_ref[1]) + e % NX).astype(F32)
    before = (iota((TOK, TOK), 0) < iota((TOK, TOK), 1)).astype(BF)
    slot = (iota((DEST * SLOT, TOK), 0) % SLOT).astype(F32)
    for z in range(NZ):
        table = g_ref[z, TOK:, :TOK].astype(F32)
        hit = jnp.zeros((DEST, TOK), F32)
        for k in range(TOP):
            hit = jnp.where(table[k : k + 1, :] == ids, 1.0, hit)
        rank = dot(hit.astype(BF), before, 1, 0)
        rank = jnp.where(hit > 0.5, rank, -1.0)
        rank = jnp.broadcast_to(rank[:, None, :], (DEST, SLOT, TOK)).reshape(DEST * SLOT, TOK)
        pick = jnp.where(rank == slot, 1.0, 0.0).astype(BF)
        got = dot(pick, g_ref[z, :TOK, :], 1, 0).astype(BF)
        out_ref[:, z * SLOT : (z + 1) * SLOT, :] = got.reshape(DEST, SLOT, Q)


def both(wa_ref, wb_ref, i, h):
    cols = slice(h * Q, (h + 1) * Q)
    return jnp.concatenate([wa_ref[i, :, cols], wb_ref[i, :, cols]], axis=0)


def project(rows, wa_ref, wb_ref, i):
    total = dot(rows[0], both(wa_ref, wb_ref, i, 0), 1, 1)
    for h in range(1, NX):
        total = total + dot(rows[h], both(wa_ref, wb_ref, i, h), 1, 1)
    return total


def gates(x_ref, wa_ref, wb_ref, pre_ref, keep_ref):
    weight = x_ref[:, D:].astype(F32)[:, :1]
    rows = [x_ref[:, h * Q : (h + 1) * Q] for h in range(NX)]
    gate = project(rows, wa_ref, wb_ref, 0)
    up = project(rows, wa_ref, wb_ref, 1)
    sig = 1.0 / (1.0 + jnp.exp(-gate))
    act = gate * sig
    hidden = act * up
    pre_ref[0] = hidden
    pre_ref[1] = weight * (up * (sig * (1.0 + gate * (1.0 - sig))))
    pre_ref[2] = weight * act
    keep_ref[...] = (weight * hidden).astype(BF)


def expert(at_ref, pre_ref, d_ref, wa_ref, wb_ref, part_ref, keep_ref):
    rows = [jnp.concatenate([d_ref[y * NX + h] for y in range(NY)], axis=0) for h in range(NX)]
    raw = project(rows, wa_ref, wb_ref, 2)
    score = jnp.sum(pre_ref[0] * raw, axis=1, keepdims=True)
    keep_ref[0] = (raw * pre_ref[1]).astype(BF)
    keep_ref[1] = (raw * pre_ref[2]).astype(BF)
    for h in range(NX):
        total = dot(keep_ref[0], both(wa_ref, wb_ref, 0, h), 1, 0)
        total = total + dot(keep_ref[1], both(wa_ref, wb_ref, 1, h), 1, 0)
        part_ref[:, h * Q : (h + 1) * Q] = total.astype(BF)
    lane = iota((ROWS, TOK), 1) - 2 * at_ref[2]
    coarse = score.astype(BF).astype(F32)
    carried = jnp.where(lane == 0, coarse, jnp.where(lane == 1, score - coarse, 0.0))
    part_ref[:, D:] = carried.astype(BF)


def down_grads(do_ref, ds_ref, ho_ref, hs_ref, a_ref, b_ref, flip):
    @pl.when(pl.program_id(0) == 0)
    def _():
        flip[:, :ROWS] = ho_ref[...].T
        flip[:, ROWS:] = hs_ref[...].T

    d = jnp.concatenate([do_ref[y, 0] for y in range(NY)] + [ds_ref[y, 0] for y in range(NY)], axis=0)
    grad = dot(flip[...], d, 1, 0).astype(BF)
    a_ref[0] = grad[:FQ]
    b_ref[0] = grad[FQ:]


def gate_up_grads(xo_ref, xs_ref, ko_ref, ks_ref, a_ref, b_ref, flip):
    @pl.when(pl.program_id(0) == 0)
    def _():
        for i in range(2):
            flip[i, :, :ROWS] = ko_ref[i].T
            flip[i, :, ROWS:] = ks_ref[i].T

    x = jnp.concatenate([xo_ref[...], xs_ref[...]], axis=0)
    for i in range(2):
        grad = dot(flip[i], x, 1, 0).astype(BF)
        a_ref[i] = grad[:FQ]
        b_ref[i] = grad[FQ:]


def place(at_ref, da_ref, db_ref, a_ref, b_ref, gate_ref, up_ref, down_ref):
    odd = at_ref[3] % 2
    for out, a, b in (
        (gate_ref, a_ref[0], b_ref[0]),
        (up_ref, a_ref[1], b_ref[1]),
        (down_ref, da_ref[0], db_ref[0]),
    ):
        out[odd] = a
        out[1 - odd] = b


def combine(at_ref, table_ref, pick_ref, home_ref, out_ref):
    ids = (NX * iota((PEER, TOK), 0) + at_ref[3]).astype(F32)
    pick = pick_ref[...]
    carried = home_ref[:, D:].astype(F32)
    score = (carried[:, 0:1] + carried[:, 1:2]) + (carried[:, 2:3] + carried[:, 3:4])
    spread = jnp.sum((pick.astype(F32) * score).reshape(PEER, SLOT, TOK), axis=1)
    table = table_ref[...]
    lines = [
        jnp.sum(jnp.where(table[k : k + 1, :] == ids, spread, 0.0), axis=0, keepdims=True) for k in range(TOP)
    ]
    lines = jnp.concatenate(lines + [jnp.zeros((16 - TOP, TOK), F32)], axis=0)
    coarse = lines.astype(BF)
    fine = (lines - coarse.astype(F32)).astype(BF)
    for h in range(NX):
        out_ref[h, :TOK, :] = dot(pick, home_ref[:, h * Q : (h + 1) * Q], 0, 0).astype(BF)
        out_ref[h, TOK:, :TOK] = coarse
        out_ref[h, TOK:, TOK : 2 * TOK] = fine
        out_ref[h, TOK:, 2 * TOK :] = jnp.zeros((16, Q - 2 * TOK), BF)


def per_device(tokens, cotangent, route, prob, w_gate, w_up, w_down):
    at = jnp.stack([lax.axis_index(a) for a in ("y", "z", "c", "x")]).astype(jnp.int32)
    ix = lax.axis_index("x")
    sib = [(0, 1), (1, 0)]
    shape = jax.ShapeDtypeStruct

    def to_experts(rows):
        rows = rows.reshape(PEER, SLOT, rows.shape[1])
        rows = lax.all_to_all(rows, ("y", "z"), split_axis=0, concat_axis=0, tiled=True)
        return rows.reshape(ROWS, rows.shape[2])

    table = jnp.concatenate([route.T.astype(BF), prob.T], axis=0)
    with jax.named_scope("gather_d"):
        packed = jnp.concatenate([cotangent, jnp.pad(table, ((0, 0), (0, Q - TOK)))], axis=0)
        every = lax.all_gather(packed, "z", axis=0, tiled=False)

    with jax.named_scope("select_x"):
        xg = lax.all_gather(tokens, "x", axis=0, tiled=False)
        table = table.astype(F32)
        xs, pick = pl.pallas_call(
            select_x,
            out_shape=(shape((ROWS, WIDE), BF), shape((ROWS, TOK), BF)),
            in_specs=[SMEM, VMEM, VMEM],
            out_specs=(VMEM, VMEM),
            compiler_params=params(),
            name="select_x",
        )(at, table, xg)
        x_own = to_experts(xs)

    with jax.named_scope("select_d"):
        ds = pl.pallas_call(
            select_d,
            out_shape=shape((DEST, PIECE, Q), BF),
            in_specs=[SMEM, VMEM],
            out_specs=VMEM,
            compiler_params=params(),
            name="select_d",
        )(at, every)

    with jax.named_scope("weights_out"):
        pick, *mats = lax.optimization_barrier((pick, w_gate, w_up, w_down))
        weights = []
        for m in range(2):
            k = (ix + m) % 2
            piece = jnp.stack([lax.dynamic_index_in_dim(w, k, 0, keepdims=False) for w in mats])
            weights.append(lax.ppermute(piece, ("c", "x"), weight_pairs(m)))

    with jax.named_scope("gates"):
        x_own, ds = lax.optimization_barrier((x_own, ds))
        d_own = lax.all_to_all(ds, ("y", "x"), split_axis=0, concat_axis=0, tiled=True)
        x_sib = lax.ppermute(x_own, "c", sib)
        ahead = pl.pallas_call(
            gates,
            out_shape=(shape((3, ROWS, FH), F32), shape((ROWS, FH), BF)),
            in_specs=[VMEM] * 3,
            out_specs=(VMEM, VMEM),
            compiler_params=params(),
            name="gates",
        )
        pre_own, hid_own = ahead(x_own, *weights)
        pre_sib, hid_sib = ahead(x_sib, *weights)
        d_own, pre_own, pre_sib = lax.optimization_barrier((d_own, pre_own, pre_sib))

    with jax.named_scope("expert"):
        d_sib = lax.ppermute(d_own, "c", sib)
        run = pl.pallas_call(
            expert,
            out_shape=(shape((ROWS, WIDE), BF), shape((2, ROWS, FH), BF)),
            in_specs=[SMEM] + [VMEM] * 4,
            out_specs=(VMEM, VMEM),
            compiler_params=params(),
            name="expert",
        )
        part_sib, keep_sib = run(at, pre_sib, d_sib, *weights)
        sent = lax.ppermute(part_sib, "c", sib)
        part_own, keep_own = run(at, pre_own, d_own, *weights)
        total = (part_own.astype(F32) + sent.astype(F32)).astype(BF)
        total, hid_own, hid_sib = lax.optimization_barrier((total, hid_own, hid_sib))

    with jax.named_scope("weights_back"):
        cut = pl.BlockSpec((ROWS, Q), lambda h: (0, h))
        cut_d = pl.BlockSpec((NY, 1, PIECE, Q), lambda h: (0, h, 0, 0))
        h_spec = pl.BlockSpec((ROWS, FH), lambda h: (0, 0))
        k_spec = pl.BlockSpec((2, ROWS, FH), lambda h: (0, 0, 0))
        pieces = pl.pallas_call(
            down_grads,
            grid=(NX,),
            out_shape=(shape((1, FQ, D), BF),) * 2,
            in_specs=[cut_d, cut_d, h_spec, h_spec],
            out_specs=(pl.BlockSpec((1, FQ, Q), lambda h: (0, 0, h)),) * 2,
            scratch_shapes=[pltpu.VMEM((FH, 2 * ROWS), BF)],
            compiler_params=params(),
            name="down_grads",
        )(d_own.reshape(NY, NX, PIECE, Q), d_sib.reshape(NY, NX, PIECE, Q), hid_own, hid_sib)
        *pieces, keep_own, keep_sib = lax.optimization_barrier((*pieces, keep_own, keep_sib))
        pieces += pl.pallas_call(
            gate_up_grads,
            grid=(NX,),
            out_shape=(shape((2, FQ, D), BF),) * 2,
            in_specs=[cut, cut, k_spec, k_spec],
            out_specs=(pl.BlockSpec((2, FQ, Q), lambda h: (0, 0, h)),) * 2,
            scratch_shapes=[pltpu.VMEM((2, FH, 2 * ROWS), BF)],
            compiler_params=params(),
            name="gate_up_grads",
        )(x_own, x_sib, keep_own, keep_sib)
        back = []
        for i, g in enumerate(pieces):
            inverse = [(b, a) for a, b in weight_pairs(i % 2)]
            back.append(lax.ppermute(g, ("c", "x"), inverse))

    with jax.named_scope("tokens_back"):
        home, back[0], back[1] = lax.optimization_barrier((to_experts(total), back[0], back[1]))
        partial = pl.pallas_call(
            combine,
            out_shape=shape((NX, TOK + 16, Q), BF),
            in_specs=[SMEM, VMEM, VMEM, VMEM],
            out_specs=VMEM,
            compiler_params=params(),
            name="combine",
        )(at, table, pick, home)
        last = lax.all_to_all(partial, "x", split_axis=0, concat_axis=0, tiled=True).astype(F32)
        grad_tokens = jnp.sum(last[:, :TOK], axis=0).astype(BF)
        lines = jnp.sum(last[:, TOK : TOK + TOP, : 2 * TOK], axis=0)
        grad_prob = (lines[:, :TOK] + lines[:, TOK:]).T
    with jax.named_scope("place"):
        part_rows = FQ // 4
        grad_gate, grad_up, grad_down = pl.pallas_call(
            place,
            grid=(4,),
            out_shape=(shape((2, FQ, D), BF),) * 3,
            in_specs=[SMEM] + [pl.BlockSpec((n, part_rows, D), lambda i: (0, i, 0)) for n in (1, 1, 2, 2)],
            out_specs=(pl.BlockSpec((2, part_rows, D), lambda i: (0, i, 0)),) * 3,
            compiler_params=params(),
            name="place",
        )(at, *back)
    return (grad_tokens, grad_prob, grad_gate, grad_up, grad_down)


def solution(mesh):
    grid = Mesh(mesh.devices.reshape(NY, NZ, NC, NX), ("y", "z", "c", "x"))
    owner = ("y", "z", "c")
    wide = P(owner, "x")
    thin = P(owner, None)
    deep = P(owner, "x", None)
    return jax.shard_map(
        per_device,
        mesh=grid,
        in_specs=(wide, wide, thin, thin, deep, deep, deep),
        out_specs=(wide, thin, deep, deep, deep),
        check_vma=False,
    )
```

```python
import jax
import jax.numpy as jnp
from jax import lax
from jax.experimental import pallas as pl
from jax.experimental.pallas import tpu as pltpu
from jax.sharding import Mesh, PartitionSpec as P

BF = jnp.bfloat16
F32 = jnp.float32
NY, NZ, NC, NX = 4, 8, 2, 4
SLOT = 16
TOK = 128
TOP = 8
PEER = NY * NZ
ROWS = PEER * SLOT
Q = 512
D = NX * Q
DEST = NY * NX
PIECE = NZ * SLOT
WIDE = D + 128
FQ = 192
FH = 2 * FQ
VMEM = pl.BlockSpec(memory_space=pltpu.VMEM)
SMEM = pl.BlockSpec(memory_space=pltpu.SMEM)


def params(mib=20):
    return pltpu.CompilerParams(vmem_limit_bytes=mib * 1024 * 1024)


def dot(a, b, ca, cb):
    return lax.dot_general(a, b, (((ca,), (cb,)), ((), ())), preferred_element_type=F32)


def iota(shape, axis):
    return lax.broadcasted_iota(jnp.int32, shape, axis)


def weight_pairs(m):
    pairs = []
    for c in range(NC):
        for h in range(NX):
            k = (h + m) % 2
            pairs.append((c * NX + h, (h // 2) * NX + 2 * c + k))
    return pairs


def select_x(at_ref, table_ref, x_ref, out_ref, pick_ref):
    ids = (NX * iota((PEER, TOK), 0) + at_ref[3]).astype(F32)
    before = (iota((TOK, TOK), 0) < iota((TOK, TOK), 1)).astype(BF)
    slot = (iota((ROWS, TOK), 0) % SLOT).astype(F32)
    lane = iota((ROWS, TOK), 1)
    table = table_ref[...]
    hit = jnp.zeros((PEER, TOK), F32)
    chance = jnp.zeros((PEER, TOK), F32)
    for k in range(TOP):
        on = table[k : k + 1, :] == ids
        hit = jnp.where(on, 1.0, hit)
        chance = jnp.where(on, table[TOP + k : TOP + k + 1, :], chance)
    rank = dot(hit.astype(BF), before, 1, 0)
    rank = jnp.where(hit > 0.5, rank, -1.0)
    rank = jnp.broadcast_to(rank[:, None, :], (PEER, SLOT, TOK)).reshape(ROWS, TOK)
    chance = jnp.broadcast_to(chance[:, None, :], (PEER, SLOT, TOK)).reshape(ROWS, TOK)
    mine = rank == slot
    share = jnp.sum(jnp.where(mine, chance, 0.0), axis=1, keepdims=True)
    pick = jnp.where(mine, 1.0, 0.0).astype(BF)
    pick_ref[...] = pick
    for h in range(NX):
        out_ref[:, h * Q : (h + 1) * Q] = dot(pick, x_ref[h], 1, 0).astype(BF)
    out_ref[:, D:] = jnp.where(lane == 0, share, 0.0).astype(BF)


def select_d(at_ref, g_ref, out_ref):
    e = iota((DEST, TOK), 0)
    ids = (NX * ((e // NX) * NZ + at_ref[1]) + e % NX).astype(F32)
    before = (iota((TOK, TOK), 0) < iota((TOK, TOK), 1)).astype(BF)
    slot = (iota((DEST * SLOT, TOK), 0) % SLOT).astype(F32)
    for z in range(NZ):
        table = g_ref[z, TOK:, :TOK].astype(F32)
        hit = jnp.zeros((DEST, TOK), F32)
        for k in range(TOP):
            hit = jnp.where(table[k : k + 1, :] == ids, 1.0, hit)
        rank = dot(hit.astype(BF), before, 1, 0)
        rank = jnp.where(hit > 0.5, rank, -1.0)
        rank = jnp.broadcast_to(rank[:, None, :], (DEST, SLOT, TOK)).reshape(DEST * SLOT, TOK)
        pick = jnp.where(rank == slot, 1.0, 0.0).astype(BF)
        got = dot(pick, g_ref[z, :TOK, :], 1, 0).astype(BF)
        out_ref[:, z * SLOT : (z + 1) * SLOT, :] = got.reshape(DEST, SLOT, Q)


def both(wa_ref, wb_ref, i, h):
    cols = slice(h * Q, (h + 1) * Q)
    return jnp.concatenate([wa_ref[i, :, cols], wb_ref[i, :, cols]], axis=0)


def project(rows, wa_ref, wb_ref, i):
    total = dot(rows[0], both(wa_ref, wb_ref, i, 0), 1, 1)
    for h in range(1, NX):
        total = total + dot(rows[h], both(wa_ref, wb_ref, i, h), 1, 1)
    return total


def gates(x_ref, wa_ref, wb_ref, pre_ref, keep_ref):
    weight = x_ref[:, D:].astype(F32)[:, :1]
    rows = [x_ref[:, h * Q : (h + 1) * Q] for h in range(NX)]
    gate = project(rows, wa_ref, wb_ref, 0)
    up = project(rows, wa_ref, wb_ref, 1)
    sig = 1.0 / (1.0 + jnp.exp(-gate))
    act = gate * sig
    hidden = act * up
    pre_ref[0] = hidden
    pre_ref[1] = weight * (up * (sig * (1.0 + gate * (1.0 - sig))))
    pre_ref[2] = weight * act
    keep_ref[...] = (weight * hidden).astype(BF)


def expert(at_ref, pre_ref, d_ref, wa_ref, wb_ref, part_ref, keep_ref):
    rows = [jnp.concatenate([d_ref[y * NX + h] for y in range(NY)], axis=0) for h in range(NX)]
    raw = project(rows, wa_ref, wb_ref, 2)
    score = jnp.sum(pre_ref[0] * raw, axis=1, keepdims=True)
    keep_ref[0] = (raw * pre_ref[1]).astype(BF)
    keep_ref[1] = (raw * pre_ref[2]).astype(BF)
    for h in range(NX):
        total = dot(keep_ref[0], both(wa_ref, wb_ref, 0, h), 1, 0)
        total = total + dot(keep_ref[1], both(wa_ref, wb_ref, 1, h), 1, 0)
        part_ref[:, h * Q : (h + 1) * Q] = total.astype(BF)
    lane = iota((ROWS, TOK), 1) - 2 * at_ref[2]
    coarse = score.astype(BF).astype(F32)
    carried = jnp.where(lane == 0, coarse, jnp.where(lane == 1, score - coarse, 0.0))
    part_ref[:, D:] = carried.astype(BF)


def weight_grads(xo_ref, xs_ref, do_ref, ds_ref, ho_ref, hs_ref, ko_ref, ks_ref, a_ref, b_ref, flip):
    @pl.when(pl.program_id(0) == 0)
    def _():
        for i in range(2):
            flip[i, :, :ROWS] = ko_ref[i].T
            flip[i, :, ROWS:] = ks_ref[i].T
        flip[2, :, :ROWS] = ho_ref[...].T
        flip[2, :, ROWS:] = hs_ref[...].T

    x = jnp.concatenate([xo_ref[...], xs_ref[...]], axis=0)
    d = jnp.concatenate([do_ref[y, 0] for y in range(NY)] + [ds_ref[y, 0] for y in range(NY)], axis=0)
    for i, rows in ((0, x), (1, x), (2, d)):
        grad = dot(flip[i], rows, 1, 0).astype(BF)
        a_ref[i] = grad[:FQ]
        b_ref[i] = grad[FQ:]


def place(at_ref, a_ref, b_ref, gate_ref, up_ref, down_ref):
    odd = at_ref[3] % 2
    for i, out in enumerate((gate_ref, up_ref, down_ref)):
        out[odd] = a_ref[i]
        out[1 - odd] = b_ref[i]


def combine(at_ref, table_ref, pick_ref, home_ref, out_ref):
    ids = (NX * iota((PEER, TOK), 0) + at_ref[3]).astype(F32)
    pick = pick_ref[...]
    carried = home_ref[:, D:].astype(F32)
    score = (carried[:, 0:1] + carried[:, 1:2]) + (carried[:, 2:3] + carried[:, 3:4])
    spread = jnp.sum((pick.astype(F32) * score).reshape(PEER, SLOT, TOK), axis=1)
    table = table_ref[...]
    lines = [
        jnp.sum(jnp.where(table[k : k + 1, :] == ids, spread, 0.0), axis=0, keepdims=True) for k in range(TOP)
    ]
    lines = jnp.concatenate(lines + [jnp.zeros((16 - TOP, TOK), F32)], axis=0)
    coarse = lines.astype(BF)
    fine = (lines - coarse.astype(F32)).astype(BF)
    for h in range(NX):
        out_ref[h, :TOK, :] = dot(pick, home_ref[:, h * Q : (h + 1) * Q], 0, 0).astype(BF)
        out_ref[h, TOK:, :TOK] = coarse
        out_ref[h, TOK:, TOK : 2 * TOK] = fine
        out_ref[h, TOK:, 2 * TOK :] = jnp.zeros((16, Q - 2 * TOK), BF)


def per_device(tokens, cotangent, route, prob, w_gate, w_up, w_down):
    at = jnp.stack([lax.axis_index(a) for a in ("y", "z", "c", "x")]).astype(jnp.int32)
    ix = lax.axis_index("x")
    sib = [(0, 1), (1, 0)]
    shape = jax.ShapeDtypeStruct

    def to_experts(rows):
        rows = rows.reshape(PEER, SLOT, rows.shape[1])
        rows = lax.all_to_all(rows, ("y", "z"), split_axis=0, concat_axis=0, tiled=True)
        return rows.reshape(ROWS, rows.shape[2])

    table = jnp.concatenate([route.T.astype(BF), prob.T], axis=0)
    with jax.named_scope("gather_d"):
        packed = jnp.concatenate([cotangent, jnp.pad(table, ((0, 0), (0, Q - TOK)))], axis=0)
        every = lax.all_gather(packed, "z", axis=0, tiled=False)

    with jax.named_scope("select_x"):
        xg = lax.all_gather(tokens, "x", axis=0, tiled=False)
        table = table.astype(F32)
        xs, pick = pl.pallas_call(
            select_x,
            out_shape=(shape((ROWS, WIDE), BF), shape((ROWS, TOK), BF)),
            in_specs=[SMEM, VMEM, VMEM],
            out_specs=(VMEM, VMEM),
            compiler_params=params(),
            name="select_x",
        )(at, table, xg)
        x_own = to_experts(xs)

    with jax.named_scope("weights_out"):
        pick, *mats = lax.optimization_barrier((pick, w_gate, w_up, w_down))
        weights = []
        for m in range(2):
            k = (ix + m) % 2
            if m == 1:
                every, *mats = lax.optimization_barrier((every, *mats))
            piece = jnp.stack([lax.dynamic_index_in_dim(w, k, 0, keepdims=False) for w in mats])
            weights.append(lax.ppermute(piece, ("c", "x"), weight_pairs(m)))

    with jax.named_scope("select_d"):
        ds = pl.pallas_call(
            select_d,
            out_shape=shape((DEST, PIECE, Q), BF),
            in_specs=[SMEM, VMEM],
            out_specs=VMEM,
            compiler_params=params(),
            name="select_d",
        )(at, every)

    with jax.named_scope("gates"):
        x_own, ds, *weights = lax.optimization_barrier((x_own, ds, *weights))
        d_own = lax.all_to_all(ds, ("y", "x"), split_axis=0, concat_axis=0, tiled=True)
        x_sib = lax.ppermute(x_own, "c", sib)
        ahead = pl.pallas_call(
            gates,
            out_shape=(shape((3, ROWS, FH), F32), shape((ROWS, FH), BF)),
            in_specs=[VMEM] * 3,
            out_specs=(VMEM, VMEM),
            compiler_params=params(),
            name="gates",
        )
        pre_own, hid_own = ahead(x_own, *weights)
        pre_sib, hid_sib = ahead(x_sib, *weights)
        d_own, pre_own, pre_sib = lax.optimization_barrier((d_own, pre_own, pre_sib))

    with jax.named_scope("expert"):
        d_sib = lax.ppermute(d_own, "c", sib)
        run = pl.pallas_call(
            expert,
            out_shape=(shape((ROWS, WIDE), BF), shape((2, ROWS, FH), BF)),
            in_specs=[SMEM] + [VMEM] * 4,
            out_specs=(VMEM, VMEM),
            compiler_params=params(),
            name="expert",
        )
        part_sib, keep_sib = run(at, pre_sib, d_sib, *weights)
        sent = lax.ppermute(part_sib, "c", sib)
        part_own, keep_own = run(at, pre_own, d_own, *weights)
        total = (part_own.astype(F32) + sent.astype(F32)).astype(BF)
        total, keep_own, keep_sib = lax.optimization_barrier((total, keep_own, keep_sib))

    with jax.named_scope("weights_back"):
        cut = pl.BlockSpec((ROWS, Q), lambda h: (0, h))
        cut_d = pl.BlockSpec((NY, 1, PIECE, Q), lambda h: (0, h, 0, 0))
        h_spec = pl.BlockSpec((ROWS, FH), lambda h: (0, 0))
        k_spec = pl.BlockSpec((2, ROWS, FH), lambda h: (0, 0, 0))
        pieces = pl.pallas_call(
            weight_grads,
            grid=(NX,),
            out_shape=(shape((3, FQ, D), BF),) * 2,
            in_specs=[cut, cut, cut_d, cut_d, h_spec, h_spec, k_spec, k_spec],
            out_specs=(pl.BlockSpec((3, FQ, Q), lambda h: (0, 0, h)),) * 2,
            scratch_shapes=[pltpu.VMEM((3, FH, 2 * ROWS), BF)],
            compiler_params=params(28),
            name="weight_grads",
        )(
            x_own,
            x_sib,
            d_own.reshape(NY, NX, PIECE, Q),
            d_sib.reshape(NY, NX, PIECE, Q),
            hid_own,
            hid_sib,
            keep_own,
            keep_sib,
        )
        back = []
        for i, g in enumerate(pieces):
            inverse = [(b, a) for a, b in weight_pairs(i)]
            back.append(lax.ppermute(g, ("c", "x"), inverse))

    with jax.named_scope("tokens_back"):
        home = to_experts(total)
        partial = pl.pallas_call(
            combine,
            out_shape=shape((NX, TOK + 16, Q), BF),
            in_specs=[SMEM, VMEM, VMEM, VMEM],
            out_specs=VMEM,
            compiler_params=params(),
            name="combine",
        )(at, table, pick, home)
        last = lax.all_to_all(partial, "x", split_axis=0, concat_axis=0, tiled=True).astype(F32)
        grad_tokens = jnp.sum(last[:, :TOK], axis=0).astype(BF)
        lines = jnp.sum(last[:, TOK : TOK + TOP, : 2 * TOK], axis=0)
        grad_prob = (lines[:, :TOK] + lines[:, TOK:]).T
    with jax.named_scope("place"):
        part_rows = FQ // 4
        grad_gate, grad_up, grad_down = pl.pallas_call(
            place,
            grid=(4,),
            out_shape=(shape((2, FQ, D), BF),) * 3,
            in_specs=[SMEM] + [pl.BlockSpec((n, part_rows, D), lambda i: (0, i, 0)) for n in (3, 3)],
            out_specs=(pl.BlockSpec((2, part_rows, D), lambda i: (0, i, 0)),) * 3,
            compiler_params=params(),
            name="place",
        )(at, *back)
    return (grad_tokens, grad_prob, grad_gate, grad_up, grad_down)


def solution(mesh):
    grid = Mesh(mesh.devices.reshape(NY, NZ, NC, NX), ("y", "z", "c", "x"))
    owner = ("y", "z", "c")
    wide = P(owner, "x")
    thin = P(owner, None)
    deep = P(owner, "x", None)
    return jax.shard_map(
        per_device,
        mesh=grid,
        in_specs=(wide, wide, thin, thin, deep, deep, deep),
        out_specs=(wide, thin, deep, deep, deep),
        check_vma=False,
    )
```

```python
import jax
import jax.numpy as jnp
from jax import lax
from jax.experimental import pallas as pl
from jax.experimental.pallas import tpu as pltpu
from jax.sharding import Mesh, PartitionSpec as P

BF = jnp.bfloat16
F32 = jnp.float32
NY, NZ, NC, NX = 4, 8, 2, 4
SLOT = 16
TOK = 128
TOP = 8
PEER = NY * NZ
ROWS = PEER * SLOT
Q = 512
D = NX * Q
WIDE = D + 128
FQ = 192
FH = 2 * FQ
VMEM = pl.BlockSpec(memory_space=pltpu.VMEM)
SMEM = pl.BlockSpec(memory_space=pltpu.SMEM)


def params(mib=20):
    return pltpu.CompilerParams(vmem_limit_bytes=mib * 1024 * 1024)


def dot(a, b, ca, cb):
    return lax.dot_general(a, b, (((ca,), (cb,)), ((), ())), preferred_element_type=F32)


def iota(shape, axis):
    return lax.broadcasted_iota(jnp.int32, shape, axis)


def weight_pairs(m):
    pairs = []
    for c in range(NC):
        for h in range(NX):
            k = (h + m) % 2
            pairs.append((c * NX + h, (h // 2) * NX + 2 * c + k))
    return pairs


def select_x(at_ref, table_ref, x_ref, out_ref, pick_ref):
    ids = (NX * iota((PEER, TOK), 0) + at_ref[3]).astype(F32)
    before = (iota((TOK, TOK), 0) < iota((TOK, TOK), 1)).astype(BF)
    slot = (iota((ROWS, TOK), 0) % SLOT).astype(F32)
    lane = iota((ROWS, TOK), 1)
    table = table_ref[...]
    hit = jnp.zeros((PEER, TOK), F32)
    chance = jnp.zeros((PEER, TOK), F32)
    for k in range(TOP):
        on = table[k : k + 1, :] == ids
        hit = jnp.where(on, 1.0, hit)
        chance = jnp.where(on, table[TOP + k : TOP + k + 1, :], chance)
    rank = dot(hit.astype(BF), before, 1, 0)
    rank = jnp.where(hit > 0.5, rank, -1.0)
    rank = jnp.broadcast_to(rank[:, None, :], (PEER, SLOT, TOK)).reshape(ROWS, TOK)
    chance = jnp.broadcast_to(chance[:, None, :], (PEER, SLOT, TOK)).reshape(ROWS, TOK)
    mine = rank == slot
    share = jnp.sum(jnp.where(mine, chance, 0.0), axis=1, keepdims=True)
    pick = jnp.where(mine, 1.0, 0.0).astype(BF)
    pick_ref[...] = pick
    for h in range(NX):
        out_ref[:, h * Q : (h + 1) * Q] = dot(pick, x_ref[h], 1, 0).astype(BF)
    out_ref[:, D:] = jnp.where(lane == 0, share, 0.0).astype(BF)


def select_d(pick_ref, d_ref, out_ref):
    for h in range(NX):
        out_ref[:, h * Q : (h + 1) * Q] = dot(pick_ref[...], d_ref[h], 1, 0).astype(BF)


def both(wa_ref, wb_ref, i, h):
    cols = slice(h * Q, (h + 1) * Q)
    return jnp.concatenate([wa_ref[i, :, cols], wb_ref[i, :, cols]], axis=0)


def project(ref, wa_ref, wb_ref, i):
    total = dot(ref[:, :Q], both(wa_ref, wb_ref, i, 0), 1, 1)
    for h in range(1, NX):
        total = total + dot(ref[:, h * Q : (h + 1) * Q], both(wa_ref, wb_ref, i, h), 1, 1)
    return total


def gates(x_ref, wa_ref, wb_ref, pre_ref, keep_ref):
    weight = x_ref[:, D:].astype(F32)[:, :1]
    gate = project(x_ref, wa_ref, wb_ref, 0)
    up = project(x_ref, wa_ref, wb_ref, 1)
    sig = 1.0 / (1.0 + jnp.exp(-gate))
    act = gate * sig
    hidden = act * up
    pre_ref[0] = hidden
    pre_ref[1] = weight * (up * (sig * (1.0 + gate * (1.0 - sig))))
    pre_ref[2] = weight * act
    keep_ref[...] = (weight * hidden).astype(BF)


def expert(at_ref, pre_ref, d_ref, wa_ref, wb_ref, part_ref, keep_ref):
    raw = project(d_ref, wa_ref, wb_ref, 2)
    score = jnp.sum(pre_ref[0] * raw, axis=1, keepdims=True)
    keep_ref[0] = (raw * pre_ref[1]).astype(BF)
    keep_ref[1] = (raw * pre_ref[2]).astype(BF)
    for h in range(NX):
        total = dot(keep_ref[0], both(wa_ref, wb_ref, 0, h), 1, 0)
        total = total + dot(keep_ref[1], both(wa_ref, wb_ref, 1, h), 1, 0)
        part_ref[:, h * Q : (h + 1) * Q] = total.astype(BF)
    lane = iota((ROWS, TOK), 1) - 2 * at_ref[2]
    coarse = score.astype(BF).astype(F32)
    carried = jnp.where(lane == 0, coarse, jnp.where(lane == 1, score - coarse, 0.0))
    part_ref[:, D:] = carried.astype(BF)


def weight_grads(xo_ref, xs_ref, do_ref, ds_ref, ho_ref, hs_ref, ko_ref, ks_ref, a_ref, b_ref, flip):
    @pl.when(pl.program_id(0) == 0)
    def _():
        for i in range(2):
            flip[i, :, :ROWS] = ko_ref[i].T
            flip[i, :, ROWS:] = ks_ref[i].T
        flip[2, :, :ROWS] = ho_ref[...].T
        flip[2, :, ROWS:] = hs_ref[...].T

    x = jnp.concatenate([xo_ref[...], xs_ref[...]], axis=0)
    d = jnp.concatenate([do_ref[...], ds_ref[...]], axis=0)
    for i, rows in ((0, x), (1, x), (2, d)):
        grad = dot(flip[i], rows, 1, 0).astype(BF)
        a_ref[i] = grad[:FQ]
        b_ref[i] = grad[FQ:]


def place(at_ref, a_ref, b_ref, gate_ref, up_ref, down_ref):
    odd = at_ref[3] % 2
    for i, out in enumerate((gate_ref, up_ref, down_ref)):
        out[odd] = a_ref[i]
        out[1 - odd] = b_ref[i]


def combine(at_ref, table_ref, pick_ref, home_ref, out_ref):
    ids = (NX * iota((PEER, TOK), 0) + at_ref[3]).astype(F32)
    pick = pick_ref[...]
    carried = home_ref[:, D:].astype(F32)
    score = (carried[:, 0:1] + carried[:, 1:2]) + (carried[:, 2:3] + carried[:, 3:4])
    spread = jnp.sum((pick.astype(F32) * score).reshape(PEER, SLOT, TOK), axis=1)
    table = table_ref[...]
    lines = [
        jnp.sum(jnp.where(table[k : k + 1, :] == ids, spread, 0.0), axis=0, keepdims=True) for k in range(TOP)
    ]
    lines = jnp.concatenate(lines + [jnp.zeros((16 - TOP, TOK), F32)], axis=0)
    coarse = lines.astype(BF)
    fine = (lines - coarse.astype(F32)).astype(BF)
    for h in range(NX):
        out_ref[h, :TOK, :] = dot(pick, home_ref[:, h * Q : (h + 1) * Q], 0, 0).astype(BF)
        out_ref[h, TOK:, :TOK] = coarse
        out_ref[h, TOK:, TOK : 2 * TOK] = fine
        out_ref[h, TOK:, 2 * TOK :] = jnp.zeros((16, Q - 2 * TOK), BF)


def per_device(tokens, cotangent, route, prob, w_gate, w_up, w_down):
    at = jnp.stack([lax.axis_index(a) for a in ("y", "z", "c", "x")]).astype(jnp.int32)
    ix = lax.axis_index("x")
    sib = [(0, 1), (1, 0)]
    shape = jax.ShapeDtypeStruct

    def to_experts(rows):
        rows = rows.reshape(PEER, SLOT, rows.shape[1])
        rows = lax.all_to_all(rows, ("y", "z"), split_axis=0, concat_axis=0, tiled=True)
        return rows.reshape(ROWS, rows.shape[2])

    with jax.named_scope("select_x"):
        xg = lax.all_gather(tokens, "x", axis=0, tiled=False)
        table = jnp.concatenate([route.T.astype(F32), prob.T.astype(F32)], axis=0)
        xs, pick = pl.pallas_call(
            select_x,
            out_shape=(shape((ROWS, WIDE), BF), shape((ROWS, TOK), BF)),
            in_specs=[SMEM, VMEM, VMEM],
            out_specs=(VMEM, VMEM),
            compiler_params=params(),
            name="select_x",
        )(at, table, xg)
        x_own = to_experts(xs)

    with jax.named_scope("select_d"):
        pick, cotangent = lax.optimization_barrier((pick, cotangent))
        dg = lax.all_gather(cotangent, "x", axis=0, tiled=False)

    with jax.named_scope("weights_out"):
        dg, *mats = lax.optimization_barrier((dg, w_gate, w_up, w_down))
        weights = []
        for m in range(2):
            k = (ix + m) % 2
            piece = jnp.stack([lax.dynamic_index_in_dim(w, k, 0, keepdims=False) for w in mats])
            weights.append(lax.ppermute(piece, ("c", "x"), weight_pairs(m)))

    with jax.named_scope("select_d"):
        ds = pl.pallas_call(
            select_d,
            out_shape=shape((ROWS, D), BF),
            in_specs=[VMEM, VMEM],
            out_specs=VMEM,
            compiler_params=params(),
            name="select_d",
        )(pick, dg)

    with jax.named_scope("gates"):
        x_own, ds, weights[0] = lax.optimization_barrier((x_own, ds, weights[0]))
        d_own = to_experts(ds)
        x_sib = lax.ppermute(x_own, "c", sib)
        ahead = pl.pallas_call(
            gates,
            out_shape=(shape((3, ROWS, FH), F32), shape((ROWS, FH), BF)),
            in_specs=[VMEM] * 3,
            out_specs=(VMEM, VMEM),
            compiler_params=params(),
            name="gates",
        )
        pre_own, hid_own = ahead(x_own, *weights)
        pre_sib, hid_sib = ahead(x_sib, *weights)
        d_own, pre_own, pre_sib = lax.optimization_barrier((d_own, pre_own, pre_sib))

    with jax.named_scope("expert"):
        d_sib = lax.ppermute(d_own, "c", sib)
        run = pl.pallas_call(
            expert,
            out_shape=(shape((ROWS, WIDE), BF), shape((2, ROWS, FH), BF)),
            in_specs=[SMEM] + [VMEM] * 4,
            out_specs=(VMEM, VMEM),
            compiler_params=params(),
            name="expert",
        )
        part_sib, keep_sib = run(at, pre_sib, d_sib, *weights)
        sent = lax.ppermute(part_sib, "c", sib)
        part_own, keep_own = run(at, pre_own, d_own, *weights)
        total = (part_own.astype(F32) + sent.astype(F32)).astype(BF)
        total, keep_own, keep_sib = lax.optimization_barrier((total, keep_own, keep_sib))

    with jax.named_scope("weights_back"):
        cut = pl.BlockSpec((ROWS, Q), lambda h: (0, h))
        h_spec = pl.BlockSpec((ROWS, FH), lambda h: (0, 0))
        k_spec = pl.BlockSpec((2, ROWS, FH), lambda h: (0, 0, 0))
        o_spec = pl.BlockSpec((3, FQ, Q), lambda h: (0, 0, h))
        pieces = pl.pallas_call(
            weight_grads,
            grid=(NX,),
            out_shape=(shape((3, FQ, D), BF),) * 2,
            in_specs=[cut] * 4 + [h_spec, h_spec, k_spec, k_spec],
            out_specs=(o_spec, o_spec),
            scratch_shapes=[pltpu.VMEM((3, FH, 2 * ROWS), BF)],
            compiler_params=params(60),
            name="weight_grads",
        )(x_own, x_sib, d_own, d_sib, hid_own, hid_sib, keep_own, keep_sib)
        back = []
        for m, g in enumerate(pieces):
            inverse = [(b, a) for a, b in weight_pairs(m)]
            back.append(lax.ppermute(g, ("c", "x"), inverse))
        part_rows = FQ // 4
        grad_gate, grad_up, grad_down = pl.pallas_call(
            place,
            grid=(4,),
            out_shape=(shape((2, FQ, D), BF),) * 3,
            in_specs=[SMEM] + [pl.BlockSpec((3, part_rows, D), lambda i: (0, i, 0))] * 2,
            out_specs=(pl.BlockSpec((2, part_rows, D), lambda i: (0, i, 0)),) * 3,
            compiler_params=params(),
            name="place",
        )(at, *back)

    with jax.named_scope("tokens_back"):
        home = to_experts(total)
        partial = pl.pallas_call(
            combine,
            out_shape=shape((NX, TOK + 16, Q), BF),
            in_specs=[SMEM, VMEM, VMEM, VMEM],
            out_specs=VMEM,
            compiler_params=params(),
            name="combine",
        )(at, table, pick, home)
        last = lax.all_to_all(partial, "x", split_axis=0, concat_axis=0, tiled=True).astype(F32)
        grad_tokens = jnp.sum(last[:, :TOK], axis=0).astype(BF)
        lines = jnp.sum(last[:, TOK : TOK + TOP, : 2 * TOK], axis=0)
        grad_prob = (lines[:, :TOK] + lines[:, TOK:]).T
    return (grad_tokens, grad_prob, grad_gate, grad_up, grad_down)


def solution(mesh):
    grid = Mesh(mesh.devices.reshape(NY, NZ, NC, NX), ("y", "z", "c", "x"))
    owner = ("y", "z", "c")
    wide = P(owner, "x")
    thin = P(owner, None)
    deep = P(owner, "x", None)
    return jax.shard_map(
        per_device,
        mesh=grid,
        in_specs=(wide, wide, thin, thin, deep, deep, deep),
        out_specs=(wide, thin, deep, deep, deep),
        check_vma=False,
    )
```

```python
import jax
import jax.numpy as jnp
from jax import lax
from jax.experimental import pallas as pl
from jax.experimental.pallas import tpu as pltpu
from jax.sharding import Mesh, PartitionSpec as P

BF = jnp.bfloat16
F32 = jnp.float32
NY, NZ, NC, NX = 4, 8, 2, 4
SLOT = 16
TOK = 128
TOP = 8
PEER = NY * NZ
ROWS = PEER * SLOT
Q = 512
D = NX * Q
WIDE = D + 128
FQ = 192
FH = 2 * FQ
VMEM = pl.BlockSpec(memory_space=pltpu.VMEM)
SMEM = pl.BlockSpec(memory_space=pltpu.SMEM)


def params(mib=20):
    return pltpu.CompilerParams(vmem_limit_bytes=mib * 1024 * 1024)


def dot(a, b, ca, cb):
    return lax.dot_general(a, b, (((ca,), (cb,)), ((), ())), preferred_element_type=F32)


def iota(shape, axis):
    return lax.broadcasted_iota(jnp.int32, shape, axis)


def weight_pairs(m):
    pairs = []
    for c in range(NC):
        for h in range(NX):
            k = (h + m) % 2
            pairs.append((c * NX + h, (h // 2) * NX + 2 * c + k))
    return pairs


def select_x(at_ref, table_ref, x_ref, out_ref, pick_ref):
    ids = (NX * iota((PEER, TOK), 0) + at_ref[3]).astype(F32)
    before = (iota((TOK, TOK), 0) < iota((TOK, TOK), 1)).astype(BF)
    slot = (iota((ROWS, TOK), 0) % SLOT).astype(F32)
    lane = iota((ROWS, TOK), 1)
    table = table_ref[...]
    hit = jnp.zeros((PEER, TOK), F32)
    chance = jnp.zeros((PEER, TOK), F32)
    for k in range(TOP):
        on = table[k : k + 1, :] == ids
        hit = jnp.where(on, 1.0, hit)
        chance = jnp.where(on, table[TOP + k : TOP + k + 1, :], chance)
    rank = dot(hit.astype(BF), before, 1, 0)
    rank = jnp.where(hit > 0.5, rank, -1.0)
    rank = jnp.broadcast_to(rank[:, None, :], (PEER, SLOT, TOK)).reshape(ROWS, TOK)
    chance = jnp.broadcast_to(chance[:, None, :], (PEER, SLOT, TOK)).reshape(ROWS, TOK)
    mine = rank == slot
    share = jnp.sum(jnp.where(mine, chance, 0.0), axis=1, keepdims=True)
    pick = jnp.where(mine, 1.0, 0.0).astype(BF)
    pick_ref[...] = pick
    for h in range(NX):
        out_ref[:, h * Q : (h + 1) * Q] = dot(pick, x_ref[h], 1, 0).astype(BF)
    out_ref[:, D:] = jnp.where(lane == 0, share, 0.0).astype(BF)


def select_d(pick_ref, d_ref, out_ref):
    for h in range(NX):
        out_ref[:, h * Q : (h + 1) * Q] = dot(pick_ref[...], d_ref[h], 1, 0).astype(BF)


def both(wa_ref, wb_ref, i, h):
    cols = slice(h * Q, (h + 1) * Q)
    return jnp.concatenate([wa_ref[i, :, cols], wb_ref[i, :, cols]], axis=0)


def project(ref, wa_ref, wb_ref, i):
    total = dot(ref[:, :Q], both(wa_ref, wb_ref, i, 0), 1, 1)
    for h in range(1, NX):
        total = total + dot(ref[:, h * Q : (h + 1) * Q], both(wa_ref, wb_ref, i, h), 1, 1)
    return total


def gates(x_ref, wa_ref, wb_ref, pre_ref, keep_ref):
    weight = x_ref[:, D:].astype(F32)[:, :1]
    gate = project(x_ref, wa_ref, wb_ref, 0)
    up = project(x_ref, wa_ref, wb_ref, 1)
    sig = 1.0 / (1.0 + jnp.exp(-gate))
    act = gate * sig
    hidden = act * up
    pre_ref[0] = hidden
    pre_ref[1] = weight * (up * (sig * (1.0 + gate * (1.0 - sig))))
    pre_ref[2] = weight * act
    keep_ref[...] = (weight * hidden).astype(BF)


def expert(at_ref, pre_ref, d_ref, wa_ref, wb_ref, da_ref, db_ref, part_ref, keep_ref):
    raw = project(d_ref, da_ref, db_ref, 0)
    score = jnp.sum(pre_ref[0] * raw, axis=1, keepdims=True)
    keep_ref[0] = (raw * pre_ref[1]).astype(BF)
    keep_ref[1] = (raw * pre_ref[2]).astype(BF)
    for h in range(NX):
        total = dot(keep_ref[0], both(wa_ref, wb_ref, 0, h), 1, 0)
        total = total + dot(keep_ref[1], both(wa_ref, wb_ref, 1, h), 1, 0)
        part_ref[:, h * Q : (h + 1) * Q] = total.astype(BF)
    lane = iota((ROWS, TOK), 1) - 2 * at_ref[2]
    coarse = score.astype(BF).astype(F32)
    carried = jnp.where(lane == 0, coarse, jnp.where(lane == 1, score - coarse, 0.0))
    part_ref[:, D:] = carried.astype(BF)


def down_grads(do_ref, ds_ref, ho_ref, hs_ref, a_ref, b_ref, flip):
    @pl.when(pl.program_id(0) == 0)
    def _():
        flip[:, :ROWS] = ho_ref[...].T
        flip[:, ROWS:] = hs_ref[...].T

    grad = dot(flip[...], jnp.concatenate([do_ref[...], ds_ref[...]], axis=0), 1, 0).astype(BF)
    a_ref[0] = grad[:FQ]
    b_ref[0] = grad[FQ:]


def gate_up_grads(xo_ref, xs_ref, ko_ref, ks_ref, a_ref, b_ref, flip):
    @pl.when(pl.program_id(0) == 0)
    def _():
        for i in range(2):
            flip[i, :, :ROWS] = ko_ref[i].T
            flip[i, :, ROWS:] = ks_ref[i].T

    x = jnp.concatenate([xo_ref[...], xs_ref[...]], axis=0)
    for i in range(2):
        grad = dot(flip[i], x, 1, 0).astype(BF)
        a_ref[i] = grad[:FQ]
        b_ref[i] = grad[FQ:]


def place(at_ref, da_ref, db_ref, a_ref, b_ref, gate_ref, up_ref, down_ref):
    odd = at_ref[3] % 2
    for out, a, b in (
        (gate_ref, a_ref[0], b_ref[0]),
        (up_ref, a_ref[1], b_ref[1]),
        (down_ref, da_ref[0], db_ref[0]),
    ):
        out[odd] = a
        out[1 - odd] = b


def combine(at_ref, table_ref, pick_ref, home_ref, out_ref):
    ids = (NX * iota((PEER, TOK), 0) + at_ref[3]).astype(F32)
    pick = pick_ref[...]
    carried = home_ref[:, D:].astype(F32)
    score = (carried[:, 0:1] + carried[:, 1:2]) + (carried[:, 2:3] + carried[:, 3:4])
    spread = jnp.sum((pick.astype(F32) * score).reshape(PEER, SLOT, TOK), axis=1)
    table = table_ref[...]
    lines = [
        jnp.sum(jnp.where(table[k : k + 1, :] == ids, spread, 0.0), axis=0, keepdims=True) for k in range(TOP)
    ]
    lines = jnp.concatenate(lines + [jnp.zeros((16 - TOP, TOK), F32)], axis=0)
    coarse = lines.astype(BF)
    fine = (lines - coarse.astype(F32)).astype(BF)
    for h in range(NX):
        out_ref[h, :TOK, :] = dot(pick, home_ref[:, h * Q : (h + 1) * Q], 0, 0).astype(BF)
        out_ref[h, TOK:, :TOK] = coarse
        out_ref[h, TOK:, TOK : 2 * TOK] = fine
        out_ref[h, TOK:, 2 * TOK :] = jnp.zeros((16, Q - 2 * TOK), BF)


def per_device(tokens, cotangent, route, prob, w_gate, w_up, w_down):
    at = jnp.stack([lax.axis_index(a) for a in ("y", "z", "c", "x")]).astype(jnp.int32)
    ix = lax.axis_index("x")
    sib = [(0, 1), (1, 0)]
    shape = jax.ShapeDtypeStruct

    def to_experts(rows):
        rows = rows.reshape(PEER, SLOT, rows.shape[1])
        rows = lax.all_to_all(rows, ("y", "z"), split_axis=0, concat_axis=0, tiled=True)
        return rows.reshape(ROWS, rows.shape[2])

    with jax.named_scope("select_x"):
        xg = lax.all_gather(tokens, "x", axis=0, tiled=False)
        table = jnp.concatenate([route.T.astype(F32), prob.T.astype(F32)], axis=0)
        xs, pick = pl.pallas_call(
            select_x,
            out_shape=(shape((ROWS, WIDE), BF), shape((ROWS, TOK), BF)),
            in_specs=[SMEM, VMEM, VMEM],
            out_specs=(VMEM, VMEM),
            compiler_params=params(),
            name="select_x",
        )(at, table, xg)
        x_own = to_experts(xs)

    with jax.named_scope("select_d"):
        pick, cotangent = lax.optimization_barrier((pick, cotangent))
        dg = lax.all_gather(cotangent, "x", axis=0, tiled=False)

    with jax.named_scope("weights_out"):
        dg, *mats = lax.optimization_barrier((dg, w_gate, w_up, w_down))
        weights = []
        for m, which in ((0, mats[:2]), (1, mats[:2]), (0, mats[2:]), (1, mats[2:])):
            k = (ix + m) % 2
            piece = jnp.stack([lax.dynamic_index_in_dim(w, k, 0, keepdims=False) for w in which])
            weights.append(lax.ppermute(piece, ("c", "x"), weight_pairs(m)))

    with jax.named_scope("select_d"):
        ds = pl.pallas_call(
            select_d,
            out_shape=shape((ROWS, D), BF),
            in_specs=[VMEM, VMEM],
            out_specs=VMEM,
            compiler_params=params(),
            name="select_d",
        )(pick, dg)

    with jax.named_scope("gates"):
        x_own, ds, weights[0] = lax.optimization_barrier((x_own, ds, weights[0]))
        d_own = to_experts(ds)
        x_sib = lax.ppermute(x_own, "c", sib)
        ahead = pl.pallas_call(
            gates,
            out_shape=(shape((3, ROWS, FH), F32), shape((ROWS, FH), BF)),
            in_specs=[VMEM] * 3,
            out_specs=(VMEM, VMEM),
            compiler_params=params(),
            name="gates",
        )
        pre_own, hid_own = ahead(x_own, *weights[:2])
        pre_sib, hid_sib = ahead(x_sib, *weights[:2])
        pre_own, pre_sib, *weights = lax.optimization_barrier((pre_own, pre_sib, *weights))
        d_own, pre_own, pre_sib = lax.optimization_barrier((d_own, pre_own, pre_sib))

    with jax.named_scope("expert"):
        d_sib = lax.ppermute(d_own, "c", sib)
        run = pl.pallas_call(
            expert,
            out_shape=(shape((ROWS, WIDE), BF), shape((2, ROWS, FH), BF)),
            in_specs=[SMEM] + [VMEM] * 6,
            out_specs=(VMEM, VMEM),
            compiler_params=params(),
            name="expert",
        )
        part_sib, keep_sib = run(at, pre_sib, d_sib, *weights)
        sent = lax.ppermute(part_sib, "c", sib)
        part_own, keep_own = run(at, pre_own, d_own, *weights)
        total = (part_own.astype(F32) + sent.astype(F32)).astype(BF)
        total, hid_own, hid_sib = lax.optimization_barrier((total, hid_own, hid_sib))

    with jax.named_scope("weights_back"):
        cut = pl.BlockSpec((ROWS, Q), lambda h: (0, h))
        h_spec = pl.BlockSpec((ROWS, FH), lambda h: (0, 0))
        k_spec = pl.BlockSpec((2, ROWS, FH), lambda h: (0, 0, 0))
        back = []

        def home_again(pieces):
            for m, piece in enumerate(pieces):
                back.append(lax.ppermute(piece, ("c", "x"), [(b, a) for a, b in weight_pairs(m)]))

        pieces = pl.pallas_call(
            down_grads,
            grid=(NX,),
            out_shape=(shape((1, FQ, D), BF),) * 2,
            in_specs=[cut, cut, h_spec, h_spec],
            out_specs=(pl.BlockSpec((1, FQ, Q), lambda h: (0, 0, h)),) * 2,
            scratch_shapes=[pltpu.VMEM((FH, 2 * ROWS), BF)],
            compiler_params=params(60),
            name="down_grads",
        )(d_own, d_sib, hid_own, hid_sib)
        *pieces, keep_own, keep_sib = lax.optimization_barrier((*pieces, keep_own, keep_sib))
        home_again(pieces)
        pieces = pl.pallas_call(
            gate_up_grads,
            grid=(NX,),
            out_shape=(shape((2, FQ, D), BF),) * 2,
            in_specs=[cut, cut, k_spec, k_spec],
            out_specs=(pl.BlockSpec((2, FQ, Q), lambda h: (0, 0, h)),) * 2,
            scratch_shapes=[pltpu.VMEM((2, FH, 2 * ROWS), BF)],
            compiler_params=params(60),
            name="gate_up_grads",
        )(x_own, x_sib, keep_own, keep_sib)
        *pieces, back[0], back[1] = lax.optimization_barrier((*pieces, back[0], back[1]))
        home_again(pieces)
        part_rows = FQ // 4
        grad_gate, grad_up, grad_down = pl.pallas_call(
            place,
            grid=(4,),
            out_shape=(shape((2, FQ, D), BF),) * 3,
            in_specs=[SMEM] + [pl.BlockSpec((n, part_rows, D), lambda i: (0, i, 0)) for n in (1, 1, 2, 2)],
            out_specs=(pl.BlockSpec((2, part_rows, D), lambda i: (0, i, 0)),) * 3,
            compiler_params=params(),
            name="place",
        )(at, *back)

    with jax.named_scope("tokens_back"):
        home = to_experts(total)
        partial = pl.pallas_call(
            combine,
            out_shape=shape((NX, TOK + 16, Q), BF),
            in_specs=[SMEM, VMEM, VMEM, VMEM],
            out_specs=VMEM,
            compiler_params=params(),
            name="combine",
        )(at, table, pick, home)
        last = lax.all_to_all(partial, "x", split_axis=0, concat_axis=0, tiled=True).astype(F32)
        grad_tokens = jnp.sum(last[:, :TOK], axis=0).astype(BF)
        lines = jnp.sum(last[:, TOK : TOK + TOP, : 2 * TOK], axis=0)
        grad_prob = (lines[:, :TOK] + lines[:, TOK:]).T
    return (grad_tokens, grad_prob, grad_gate, grad_up, grad_down)


def solution(mesh):
    grid = Mesh(mesh.devices.reshape(NY, NZ, NC, NX), ("y", "z", "c", "x"))
    owner = ("y", "z", "c")
    wide = P(owner, "x")
    thin = P(owner, None)
    deep = P(owner, "x", None)
    return jax.shard_map(
        per_device,
        mesh=grid,
        in_specs=(wide, wide, thin, thin, deep, deep, deep),
        out_specs=(wide, thin, deep, deep, deep),
        check_vma=False,
    )
```

```python
import jax
import jax.numpy as jnp
from jax import lax
from jax.experimental import pallas as pl
from jax.experimental.pallas import tpu as pltpu
from jax.sharding import Mesh, PartitionSpec as P

BF = jnp.bfloat16
F32 = jnp.float32
NY, NZ, NC, NX = 4, 8, 2, 4
SLOT = 16
TOK = 128
TOP = 8
PEER = NY * NZ
ROWS = PEER * SLOT
Q = 512
D = NX * Q
WIDE = D + 128
FQ = 192
FH = 2 * FQ
VMEM = pl.BlockSpec(memory_space=pltpu.VMEM)
SMEM = pl.BlockSpec(memory_space=pltpu.SMEM)


def params(mib=20):
    return pltpu.CompilerParams(vmem_limit_bytes=mib * 1024 * 1024)


def dot(a, b, ca, cb):
    return lax.dot_general(a, b, (((ca,), (cb,)), ((), ())), preferred_element_type=F32)


def iota(shape, axis):
    return lax.broadcasted_iota(jnp.int32, shape, axis)


def weight_pairs(m):
    pairs = []
    for c in range(NC):
        for h in range(NX):
            k = (h + m) % 2
            pairs.append((c * NX + h, (h // 2) * NX + 2 * c + k))
    return pairs


def select_x(at_ref, table_ref, x_ref, out_ref, pick_ref):
    ids = (NX * iota((PEER, TOK), 0) + at_ref[3]).astype(F32)
    before = (iota((TOK, TOK), 0) < iota((TOK, TOK), 1)).astype(BF)
    slot = (iota((ROWS, TOK), 0) % SLOT).astype(F32)
    lane = iota((ROWS, TOK), 1)
    table = table_ref[...]
    hit = jnp.zeros((PEER, TOK), F32)
    chance = jnp.zeros((PEER, TOK), F32)
    for k in range(TOP):
        on = table[k : k + 1, :] == ids
        hit = jnp.where(on, 1.0, hit)
        chance = jnp.where(on, table[TOP + k : TOP + k + 1, :], chance)
    rank = dot(hit.astype(BF), before, 1, 0)
    rank = jnp.where(hit > 0.5, rank, -1.0)
    rank = jnp.broadcast_to(rank[:, None, :], (PEER, SLOT, TOK)).reshape(ROWS, TOK)
    chance = jnp.broadcast_to(chance[:, None, :], (PEER, SLOT, TOK)).reshape(ROWS, TOK)
    mine = rank == slot
    share = jnp.sum(jnp.where(mine, chance, 0.0), axis=1, keepdims=True)
    pick = jnp.where(mine, 1.0, 0.0).astype(BF)
    pick_ref[...] = pick
    for h in range(NX):
        out_ref[:, h * Q : (h + 1) * Q] = dot(pick, x_ref[h], 1, 0).astype(BF)
    out_ref[:, D:] = jnp.where(lane == 0, share, 0.0).astype(BF)


def select_d(pick_ref, d_ref, out_ref):
    for h in range(NX):
        out_ref[:, h * Q : (h + 1) * Q] = dot(pick_ref[...], d_ref[h], 1, 0).astype(BF)


def both(wa_ref, wb_ref, i, h):
    cols = slice(h * Q, (h + 1) * Q)
    return jnp.concatenate([wa_ref[i, :, cols], wb_ref[i, :, cols]], axis=0)


def project(ref, wa_ref, wb_ref, i):
    total = dot(ref[:, :Q], both(wa_ref, wb_ref, i, 0), 1, 1)
    for h in range(1, NX):
        total = total + dot(ref[:, h * Q : (h + 1) * Q], both(wa_ref, wb_ref, i, h), 1, 1)
    return total


def gates(x_ref, wa_ref, wb_ref, pre_ref, keep_ref):
    weight = x_ref[:, D:].astype(F32)[:, :1]
    gate = project(x_ref, wa_ref, wb_ref, 0)
    up = project(x_ref, wa_ref, wb_ref, 1)
    sig = 1.0 / (1.0 + jnp.exp(-gate))
    act = gate * sig
    hidden = act * up
    pre_ref[0] = hidden
    pre_ref[1] = weight * (up * (sig * (1.0 + gate * (1.0 - sig))))
    pre_ref[2] = weight * act
    keep_ref[...] = (weight * hidden).astype(BF)


def expert(at_ref, pre_ref, d_ref, wa_ref, wb_ref, da_ref, db_ref, part_ref, keep_ref):
    raw = project(d_ref, da_ref, db_ref, 0)
    score = jnp.sum(pre_ref[0] * raw, axis=1, keepdims=True)
    keep_ref[0] = (raw * pre_ref[1]).astype(BF)
    keep_ref[1] = (raw * pre_ref[2]).astype(BF)
    for h in range(NX):
        total = dot(keep_ref[0], both(wa_ref, wb_ref, 0, h), 1, 0)
        total = total + dot(keep_ref[1], both(wa_ref, wb_ref, 1, h), 1, 0)
        part_ref[:, h * Q : (h + 1) * Q] = total.astype(BF)
    lane = iota((ROWS, TOK), 1) - 2 * at_ref[2]
    coarse = score.astype(BF).astype(F32)
    carried = jnp.where(lane == 0, coarse, jnp.where(lane == 1, score - coarse, 0.0))
    part_ref[:, D:] = carried.astype(BF)


def down_grads(do_ref, ds_ref, ho_ref, hs_ref, a_ref, b_ref, flip):
    @pl.when(pl.program_id(0) == 0)
    def _():
        flip[:, :ROWS] = ho_ref[...].T
        flip[:, ROWS:] = hs_ref[...].T

    grad = dot(flip[...], jnp.concatenate([do_ref[...], ds_ref[...]], axis=0), 1, 0).astype(BF)
    a_ref[0] = grad[:FQ]
    b_ref[0] = grad[FQ:]


def gate_up_grads(xo_ref, xs_ref, ko_ref, ks_ref, a_ref, b_ref, flip):
    @pl.when(pl.program_id(0) == 0)
    def _():
        for i in range(2):
            flip[i, :, :ROWS] = ko_ref[i].T
            flip[i, :, ROWS:] = ks_ref[i].T

    x = jnp.concatenate([xo_ref[...], xs_ref[...]], axis=0)
    for i in range(2):
        grad = dot(flip[i], x, 1, 0).astype(BF)
        a_ref[i] = grad[:FQ]
        b_ref[i] = grad[FQ:]


def place(at_ref, da_ref, db_ref, a_ref, b_ref, gate_ref, up_ref, down_ref):
    odd = at_ref[3] % 2
    for out, a, b in (
        (gate_ref, a_ref[0], b_ref[0]),
        (up_ref, a_ref[1], b_ref[1]),
        (down_ref, da_ref[0], db_ref[0]),
    ):
        out[odd] = a
        out[1 - odd] = b


def combine(at_ref, table_ref, pick_ref, home_ref, out_ref):
    ids = (NX * iota((PEER, TOK), 0) + at_ref[3]).astype(F32)
    pick = pick_ref[...]
    carried = home_ref[:, D:].astype(F32)
    score = (carried[:, 0:1] + carried[:, 1:2]) + (carried[:, 2:3] + carried[:, 3:4])
    spread = jnp.sum((pick.astype(F32) * score).reshape(PEER, SLOT, TOK), axis=1)
    table = table_ref[...]
    lines = [
        jnp.sum(jnp.where(table[k : k + 1, :] == ids, spread, 0.0), axis=0, keepdims=True) for k in range(TOP)
    ]
    lines = jnp.concatenate(lines + [jnp.zeros((16 - TOP, TOK), F32)], axis=0)
    coarse = lines.astype(BF)
    fine = (lines - coarse.astype(F32)).astype(BF)
    for h in range(NX):
        out_ref[h, :TOK, :] = dot(pick, home_ref[:, h * Q : (h + 1) * Q], 0, 0).astype(BF)
        out_ref[h, TOK:, :TOK] = coarse
        out_ref[h, TOK:, TOK : 2 * TOK] = fine
        out_ref[h, TOK:, 2 * TOK :] = jnp.zeros((16, Q - 2 * TOK), BF)


def per_device(tokens, cotangent, route, prob, w_gate, w_up, w_down):
    at = jnp.stack([lax.axis_index(a) for a in ("y", "z", "c", "x")]).astype(jnp.int32)
    ix = lax.axis_index("x")
    sib = [(0, 1), (1, 0)]
    shape = jax.ShapeDtypeStruct

    def to_experts(rows):
        rows = rows.reshape(PEER, SLOT, rows.shape[1])
        rows = lax.all_to_all(rows, ("y", "z"), split_axis=0, concat_axis=0, tiled=True)
        return rows.reshape(ROWS, rows.shape[2])

    with jax.named_scope("select_x"):
        xg = lax.all_gather(tokens, "x", axis=0, tiled=False)
        table = jnp.concatenate([route.T.astype(F32), prob.T.astype(F32)], axis=0)
        xs, pick = pl.pallas_call(
            select_x,
            out_shape=(shape((ROWS, WIDE), BF), shape((ROWS, TOK), BF)),
            in_specs=[SMEM, VMEM, VMEM],
            out_specs=(VMEM, VMEM),
            compiler_params=params(),
            name="select_x",
        )(at, table, xg)
        x_own = to_experts(xs)

    with jax.named_scope("select_d"):
        pick, cotangent = lax.optimization_barrier((pick, cotangent))
        dg = lax.all_gather(cotangent, "x", axis=0, tiled=False)

    with jax.named_scope("weights_out"):
        dg, *mats = lax.optimization_barrier((dg, w_gate, w_up, w_down))
        weights = []
        for m, which in ((0, mats[:2]), (1, mats[:2]), (0, mats[2:]), (1, mats[2:])):
            k = (ix + m) % 2
            piece = jnp.stack([lax.dynamic_index_in_dim(w, k, 0, keepdims=False) for w in which])
            weights.append(lax.ppermute(piece, ("c", "x"), weight_pairs(m)))

    with jax.named_scope("select_d"):
        ds = pl.pallas_call(
            select_d,
            out_shape=shape((ROWS, D), BF),
            in_specs=[VMEM, VMEM],
            out_specs=VMEM,
            compiler_params=params(),
            name="select_d",
        )(pick, dg)

    with jax.named_scope("gates"):
        x_own, ds, weights[0] = lax.optimization_barrier((x_own, ds, weights[0]))
        d_own = to_experts(ds)
        x_sib = lax.ppermute(x_own, "c", sib)
        ahead = pl.pallas_call(
            gates,
            out_shape=(shape((3, ROWS, FH), F32), shape((ROWS, FH), BF)),
            in_specs=[VMEM] * 3,
            out_specs=(VMEM, VMEM),
            compiler_params=params(),
            name="gates",
        )
        pre_own, hid_own = ahead(x_own, *weights[:2])
        pre_sib, hid_sib = ahead(x_sib, *weights[:2])
        pre_own, pre_sib, *weights = lax.optimization_barrier((pre_own, pre_sib, *weights))
        d_own, pre_own, pre_sib = lax.optimization_barrier((d_own, pre_own, pre_sib))

    with jax.named_scope("expert"):
        d_sib = lax.ppermute(d_own, "c", sib)
        run = pl.pallas_call(
            expert,
            out_shape=(shape((ROWS, WIDE), BF), shape((2, ROWS, FH), BF)),
            in_specs=[SMEM] + [VMEM] * 6,
            out_specs=(VMEM, VMEM),
            compiler_params=params(),
            name="expert",
        )
        part_own, keep_own = run(at, pre_own, d_own, *weights)
        part_own, d_sib = lax.optimization_barrier((part_own, d_sib))
        part_sib, keep_sib = run(at, pre_sib, d_sib, *weights)
        part_sib, hid_own, hid_sib = lax.optimization_barrier((part_sib, hid_own, hid_sib))
        sent = lax.ppermute(part_sib, "c", sib)

    with jax.named_scope("weights_back"):
        cut = pl.BlockSpec((ROWS, Q), lambda h: (0, h))
        h_spec = pl.BlockSpec((ROWS, FH), lambda h: (0, 0))
        k_spec = pl.BlockSpec((2, ROWS, FH), lambda h: (0, 0, 0))
        back = []

        def home_again(pieces):
            for m, piece in enumerate(pieces):
                back.append(lax.ppermute(piece, ("c", "x"), [(b, a) for a, b in weight_pairs(m)]))

        pieces = pl.pallas_call(
            down_grads,
            grid=(NX,),
            out_shape=(shape((1, FQ, D), BF),) * 2,
            in_specs=[cut, cut, h_spec, h_spec],
            out_specs=(pl.BlockSpec((1, FQ, Q), lambda h: (0, 0, h)),) * 2,
            scratch_shapes=[pltpu.VMEM((FH, 2 * ROWS), BF)],
            compiler_params=params(),
            name="down_grads",
        )(d_own, d_sib, hid_own, hid_sib)
        *pieces, sent = lax.optimization_barrier((*pieces, sent))
        home_again(pieces)
        total = (part_own.astype(F32) + sent.astype(F32)).astype(BF)
        total, keep_own, keep_sib = lax.optimization_barrier((total, keep_own, keep_sib))
        pieces = pl.pallas_call(
            gate_up_grads,
            grid=(NX,),
            out_shape=(shape((2, FQ, D), BF),) * 2,
            in_specs=[cut, cut, k_spec, k_spec],
            out_specs=(pl.BlockSpec((2, FQ, Q), lambda h: (0, 0, h)),) * 2,
            scratch_shapes=[pltpu.VMEM((2, FH, 2 * ROWS), BF)],
            compiler_params=params(60),
            name="gate_up_grads",
        )(x_own, x_sib, keep_own, keep_sib)
        *pieces, back[0], back[1] = lax.optimization_barrier((*pieces, back[0], back[1]))
        home_again(pieces)
        part_rows = FQ // 4
        grad_gate, grad_up, grad_down = pl.pallas_call(
            place,
            grid=(4,),
            out_shape=(shape((2, FQ, D), BF),) * 3,
            in_specs=[SMEM] + [pl.BlockSpec((n, part_rows, D), lambda i: (0, i, 0)) for n in (1, 1, 2, 2)],
            out_specs=(pl.BlockSpec((2, part_rows, D), lambda i: (0, i, 0)),) * 3,
            compiler_params=params(),
            name="place",
        )(at, *back)

    with jax.named_scope("tokens_back"):
        home = to_experts(total)
        partial = pl.pallas_call(
            combine,
            out_shape=shape((NX, TOK + 16, Q), BF),
            in_specs=[SMEM, VMEM, VMEM, VMEM],
            out_specs=VMEM,
            compiler_params=params(),
            name="combine",
        )(at, table, pick, home)
        last = lax.all_to_all(partial, "x", split_axis=0, concat_axis=0, tiled=True).astype(F32)
        grad_tokens = jnp.sum(last[:, :TOK], axis=0).astype(BF)
        lines = jnp.sum(last[:, TOK : TOK + TOP, : 2 * TOK], axis=0)
        grad_prob = (lines[:, :TOK] + lines[:, TOK:]).T
    return (grad_tokens, grad_prob, grad_gate, grad_up, grad_down)


def solution(mesh):
    grid = Mesh(mesh.devices.reshape(NY, NZ, NC, NX), ("y", "z", "c", "x"))
    owner = ("y", "z", "c")
    wide = P(owner, "x")
    thin = P(owner, None)
    deep = P(owner, "x", None)
    return jax.shard_map(
        per_device,
        mesh=grid,
        in_specs=(wide, wide, thin, thin, deep, deep, deep),
        out_specs=(wide, thin, deep, deep, deep),
        check_vma=False,
    )
```

```python
import jax
import jax.numpy as jnp
from jax import lax
from jax.experimental import pallas as pl
from jax.experimental.pallas import tpu as pltpu
from jax.sharding import Mesh, PartitionSpec as P

BF = jnp.bfloat16
F32 = jnp.float32
NY, NZ, NC, NX = 4, 8, 2, 4
SLOT = 16
TOK = 128
TOP = 8
PEER = NY * NZ
ROWS = PEER * SLOT
Q = 512
D = NX * Q
WIDE = D + 128
FQ = 192
FH = 2 * FQ
COST = 100_000_000_000
VMEM = pl.BlockSpec(memory_space=pltpu.VMEM)
SMEM = pl.BlockSpec(memory_space=pltpu.SMEM)


def params(mib=20):
    return pltpu.CompilerParams(vmem_limit_bytes=mib * 1024 * 1024)


def dot(a, b, ca, cb):
    return lax.dot_general(a, b, (((ca,), (cb,)), ((), ())), preferred_element_type=F32)


def iota(shape, axis):
    return lax.broadcasted_iota(jnp.int32, shape, axis)


def weight_pairs(m):
    pairs = []
    for c in range(NC):
        for h in range(NX):
            k = (h + m) % 2
            pairs.append((c * NX + h, (h // 2) * NX + 2 * c + k))
    return pairs


def select_x(at_ref, table_ref, x_ref, out_ref, pick_ref):
    ids = (NX * iota((PEER, TOK), 0) + at_ref[3]).astype(F32)
    before = (iota((TOK, TOK), 0) < iota((TOK, TOK), 1)).astype(BF)
    slot = (iota((ROWS, TOK), 0) % SLOT).astype(F32)
    lane = iota((ROWS, TOK), 1)
    table = table_ref[...]
    hit = jnp.zeros((PEER, TOK), F32)
    chance = jnp.zeros((PEER, TOK), F32)
    for k in range(TOP):
        on = table[k : k + 1, :] == ids
        hit = jnp.where(on, 1.0, hit)
        chance = jnp.where(on, table[TOP + k : TOP + k + 1, :], chance)
    rank = dot(hit.astype(BF), before, 1, 0)
    rank = jnp.where(hit > 0.5, rank, -1.0)
    rank = jnp.broadcast_to(rank[:, None, :], (PEER, SLOT, TOK)).reshape(ROWS, TOK)
    chance = jnp.broadcast_to(chance[:, None, :], (PEER, SLOT, TOK)).reshape(ROWS, TOK)
    mine = rank == slot
    share = jnp.sum(jnp.where(mine, chance, 0.0), axis=1, keepdims=True)
    pick = jnp.where(mine, 1.0, 0.0).astype(BF)
    pick_ref[...] = pick
    for h in range(NX):
        out_ref[:, h * Q : (h + 1) * Q] = dot(pick, x_ref[h], 1, 0).astype(BF)
    out_ref[:, D:] = jnp.where(lane == 0, share, 0.0).astype(BF)


def select_d(pick_ref, d_ref, out_ref):
    for h in range(NX):
        out_ref[:, h * Q : (h + 1) * Q] = dot(pick_ref[...], d_ref[h], 1, 0).astype(BF)


def both(wa_ref, wb_ref, i, h):
    cols = slice(h * Q, (h + 1) * Q)
    return jnp.concatenate([wa_ref[i, :, cols], wb_ref[i, :, cols]], axis=0)


def project(ref, wa_ref, wb_ref, i):
    total = dot(ref[:, :Q], both(wa_ref, wb_ref, i, 0), 1, 1)
    for h in range(1, NX):
        total = total + dot(ref[:, h * Q : (h + 1) * Q], both(wa_ref, wb_ref, i, h), 1, 1)
    return total


def gates(x_ref, wa_ref, wb_ref, pre_ref, keep_ref):
    weight = x_ref[:, D:].astype(F32)[:, :1]
    gate = project(x_ref, wa_ref, wb_ref, 0)
    up = project(x_ref, wa_ref, wb_ref, 1)
    sig = 1.0 / (1.0 + jnp.exp(-gate))
    act = gate * sig
    hidden = act * up
    pre_ref[0] = hidden
    pre_ref[1] = weight * (up * (sig * (1.0 + gate * (1.0 - sig))))
    pre_ref[2] = weight * act
    keep_ref[...] = (weight * hidden).astype(BF)


def expert(at_ref, pre_ref, d_ref, wa_ref, wb_ref, da_ref, db_ref, part_ref, keep_ref):
    raw = project(d_ref, da_ref, db_ref, 0)
    score = jnp.sum(pre_ref[0] * raw, axis=1, keepdims=True)
    keep_ref[0] = (raw * pre_ref[1]).astype(BF)
    keep_ref[1] = (raw * pre_ref[2]).astype(BF)
    for h in range(NX):
        total = dot(keep_ref[0], both(wa_ref, wb_ref, 0, h), 1, 0)
        total = total + dot(keep_ref[1], both(wa_ref, wb_ref, 1, h), 1, 0)
        part_ref[:, h * Q : (h + 1) * Q] = total.astype(BF)
    lane = iota((ROWS, TOK), 1) - 2 * at_ref[2]
    coarse = score.astype(BF).astype(F32)
    carried = jnp.where(lane == 0, coarse, jnp.where(lane == 1, score - coarse, 0.0))
    part_ref[:, D:] = carried.astype(BF)


def down_grads(do_ref, ds_ref, ho_ref, hs_ref, a_ref, b_ref, flip):
    @pl.when(pl.program_id(0) == 0)
    def _():
        flip[:, :ROWS] = ho_ref[...].T
        flip[:, ROWS:] = hs_ref[...].T

    grad = dot(flip[...], jnp.concatenate([do_ref[...], ds_ref[...]], axis=0), 1, 0).astype(BF)
    a_ref[0] = grad[:FQ]
    b_ref[0] = grad[FQ:]


def gate_up_grads(xo_ref, xs_ref, ko_ref, ks_ref, a_ref, b_ref, flip):
    @pl.when(pl.program_id(0) == 0)
    def _():
        for i in range(2):
            flip[i, :, :ROWS] = ko_ref[i].T
            flip[i, :, ROWS:] = ks_ref[i].T

    x = jnp.concatenate([xo_ref[...], xs_ref[...]], axis=0)
    for i in range(2):
        grad = dot(flip[i], x, 1, 0).astype(BF)
        a_ref[i] = grad[:FQ]
        b_ref[i] = grad[FQ:]


def place(at_ref, da_ref, db_ref, a_ref, b_ref, gate_ref, up_ref, down_ref):
    odd = at_ref[3] % 2
    for out, a, b in (
        (gate_ref, a_ref[0], b_ref[0]),
        (up_ref, a_ref[1], b_ref[1]),
        (down_ref, da_ref[0], db_ref[0]),
    ):
        out[odd] = a
        out[1 - odd] = b


def combine(at_ref, table_ref, pick_ref, home_ref, out_ref):
    ids = (NX * iota((PEER, TOK), 0) + at_ref[3]).astype(F32)
    pick = pick_ref[...]
    carried = home_ref[:, D:].astype(F32)
    score = (carried[:, 0:1] + carried[:, 1:2]) + (carried[:, 2:3] + carried[:, 3:4])
    spread = jnp.sum((pick.astype(F32) * score).reshape(PEER, SLOT, TOK), axis=1)
    table = table_ref[...]
    lines = [
        jnp.sum(jnp.where(table[k : k + 1, :] == ids, spread, 0.0), axis=0, keepdims=True) for k in range(TOP)
    ]
    lines = jnp.concatenate(lines + [jnp.zeros((16 - TOP, TOK), F32)], axis=0)
    coarse = lines.astype(BF)
    fine = (lines - coarse.astype(F32)).astype(BF)
    for h in range(NX):
        out_ref[h, :TOK, :] = dot(pick, home_ref[:, h * Q : (h + 1) * Q], 0, 0).astype(BF)
        out_ref[h, TOK:, :TOK] = coarse
        out_ref[h, TOK:, TOK : 2 * TOK] = fine
        out_ref[h, TOK:, 2 * TOK :] = jnp.zeros((16, Q - 2 * TOK), BF)


def per_device(tokens, cotangent, route, prob, w_gate, w_up, w_down):
    at = jnp.stack([lax.axis_index(a) for a in ("y", "z", "c", "x")]).astype(jnp.int32)
    ix = lax.axis_index("x")
    sib = [(0, 1), (1, 0)]
    shape = jax.ShapeDtypeStruct

    def to_experts(rows):
        rows = rows.reshape(PEER, SLOT, rows.shape[1])
        rows = lax.all_to_all(rows, ("y", "z"), split_axis=0, concat_axis=0, tiled=True)
        return rows.reshape(ROWS, rows.shape[2])

    with jax.named_scope("select_x"):
        xg = lax.all_gather(tokens, "x", axis=0, tiled=False)
        table = jnp.concatenate([route.T.astype(F32), prob.T.astype(F32)], axis=0)
        xs, pick = pl.pallas_call(
            select_x,
            out_shape=(shape((ROWS, WIDE), BF), shape((ROWS, TOK), BF)),
            in_specs=[SMEM, VMEM, VMEM],
            out_specs=(VMEM, VMEM),
            compiler_params=params(),
            name="select_x",
        )(at, table, xg)
        x_own = to_experts(xs)

    with jax.named_scope("select_d"):
        pick, cotangent = lax.optimization_barrier((pick, cotangent))
        dg = lax.all_gather(cotangent, "x", axis=0, tiled=False)

    with jax.named_scope("weights_out"):
        dg, *mats = lax.optimization_barrier((dg, w_gate, w_up, w_down))
        weights = []
        for m in (0, 1, 0, 1):
            k = (ix + m) % 2
            if len(weights) == 2:
                *mats, weights[1] = lax.optimization_barrier((*mats, weights[1]))
            which = mats[2:] if len(weights) > 1 else mats[:2]
            piece = jnp.stack([lax.dynamic_index_in_dim(w, k, 0, keepdims=False) for w in which])
            weights.append(lax.ppermute(piece, ("c", "x"), weight_pairs(m)))

    with jax.named_scope("select_d"):
        ds = pl.pallas_call(
            select_d,
            out_shape=shape((ROWS, D), BF),
            in_specs=[VMEM, VMEM],
            out_specs=VMEM,
            compiler_params=params(),
            name="select_d",
        )(pick, dg)

    with jax.named_scope("gates"):
        x_own, ds, weights[0] = lax.optimization_barrier((x_own, ds, weights[0]))
        d_own = to_experts(ds)
        x_sib = lax.ppermute(x_own, "c", sib)
        ahead = pl.pallas_call(
            gates,
            out_shape=(shape((3, ROWS, FH), F32), shape((ROWS, FH), BF)),
            in_specs=[VMEM] * 3,
            out_specs=(VMEM, VMEM),
            compiler_params=params(),
            name="gates",
        )
        pre_own, hid_own = ahead(x_own, *weights[:2])
        pre_sib, hid_sib = ahead(x_sib, *weights[:2])
        pre_own, pre_sib, *weights = lax.optimization_barrier((pre_own, pre_sib, *weights))
        d_own, pre_own, pre_sib = lax.optimization_barrier((d_own, pre_own, pre_sib))

    with jax.named_scope("expert"):
        d_sib = lax.ppermute(d_own, "c", sib)
        run = pl.pallas_call(
            expert,
            out_shape=(shape((ROWS, WIDE), BF), shape((2, ROWS, FH), BF)),
            in_specs=[SMEM] + [VMEM] * 6,
            out_specs=(VMEM, VMEM),
            compiler_params=params(),
            name="expert",
        )
        part_own, keep_own = run(at, pre_own, d_own, *weights)
        part_own, d_sib = lax.optimization_barrier((part_own, d_sib))
        part_sib, keep_sib = run(at, pre_sib, d_sib, *weights)
        part_sib, hid_own, hid_sib = lax.optimization_barrier((part_sib, hid_own, hid_sib))
        sent = lax.ppermute(part_sib, "c", sib)

    with jax.named_scope("weights_back"):
        cut = pl.BlockSpec((ROWS, Q), lambda h: (0, h))
        h_spec = pl.BlockSpec((ROWS, FH), lambda h: (0, 0))
        k_spec = pl.BlockSpec((2, ROWS, FH), lambda h: (0, 0, 0))
        back = []

        def home_again(pieces):
            for m, piece in enumerate(pieces):
                back.append(lax.ppermute(piece, ("c", "x"), [(b, a) for a, b in weight_pairs(m)]))

        pieces = pl.pallas_call(
            down_grads,
            grid=(NX,),
            out_shape=(shape((1, FQ, D), BF),) * 2,
            in_specs=[cut, cut, h_spec, h_spec],
            out_specs=(pl.BlockSpec((1, FQ, Q), lambda h: (0, 0, h)),) * 2,
            scratch_shapes=[pltpu.VMEM((FH, 2 * ROWS), BF)],
            compiler_params=params(),
            name="down_grads",
        )(d_own, d_sib, hid_own, hid_sib)
        *pieces, sent = lax.optimization_barrier((*pieces, sent))
        home_again(pieces)
        total = (part_own.astype(F32) + sent.astype(F32)).astype(BF)
        total, keep_own, keep_sib = lax.optimization_barrier((total, keep_own, keep_sib))
        back[0], back[1], keep_own, keep_sib = lax.optimization_barrier((back[0], back[1], keep_own, keep_sib))
        pieces = pl.pallas_call(
            gate_up_grads,
            grid=(NX,),
            out_shape=(shape((2, FQ, D), BF),) * 2,
            in_specs=[cut, cut, k_spec, k_spec],
            out_specs=(pl.BlockSpec((2, FQ, Q), lambda h: (0, 0, h)),) * 2,
            scratch_shapes=[pltpu.VMEM((2, FH, 2 * ROWS), BF)],
            cost_estimate=pl.CostEstimate(flops=COST, bytes_accessed=COST // 100, transcendentals=0),
            compiler_params=params(60),
            name="gate_up_grads",
        )(x_own, x_sib, keep_own, keep_sib)
        home_again(pieces)
        part_rows = FQ // 4
        grad_gate, grad_up, grad_down = pl.pallas_call(
            place,
            grid=(4,),
            out_shape=(shape((2, FQ, D), BF),) * 3,
            in_specs=[SMEM] + [pl.BlockSpec((n, part_rows, D), lambda i: (0, i, 0)) for n in (1, 1, 2, 2)],
            out_specs=(pl.BlockSpec((2, part_rows, D), lambda i: (0, i, 0)),) * 3,
            compiler_params=params(),
            name="place",
        )(at, *back)

    with jax.named_scope("tokens_back"):
        home = to_experts(total)
        partial = pl.pallas_call(
            combine,
            out_shape=shape((NX, TOK + 16, Q), BF),
            in_specs=[SMEM, VMEM, VMEM, VMEM],
            out_specs=VMEM,
            compiler_params=params(),
            name="combine",
        )(at, table, pick, home)
        last = lax.all_to_all(partial, "x", split_axis=0, concat_axis=0, tiled=True).astype(F32)
        grad_tokens = jnp.sum(last[:, :TOK], axis=0).astype(BF)
        lines = jnp.sum(last[:, TOK : TOK + TOP, : 2 * TOK], axis=0)
        grad_prob = (lines[:, :TOK] + lines[:, TOK:]).T
    return (grad_tokens, grad_prob, grad_gate, grad_up, grad_down)


def solution(mesh):
    grid = Mesh(mesh.devices.reshape(NY, NZ, NC, NX), ("y", "z", "c", "x"))
    owner = ("y", "z", "c")
    wide = P(owner, "x")
    thin = P(owner, None)
    deep = P(owner, "x", None)
    return jax.shard_map(
        per_device,
        mesh=grid,
        in_specs=(wide, wide, thin, thin, deep, deep, deep),
        out_specs=(wide, thin, deep, deep, deep),
        check_vma=False,
    )
```

```python
import jax
import jax.numpy as jnp
from jax import lax
from jax.experimental import pallas as pl
from jax.experimental.pallas import tpu as pltpu
from jax.sharding import Mesh, PartitionSpec as P

BF = jnp.bfloat16
F32 = jnp.float32
NY, NZ, NC, NX = 4, 8, 2, 4
SLOT = 16
TOK = 128
TOP = 8
PEER = NY * NZ
ROWS = PEER * SLOT
Q = 512
D = NX * Q
WIDE = D + 128
FQ = 192
FH = 2 * FQ
COST = 100_000_000_000
VMEM = pl.BlockSpec(memory_space=pltpu.VMEM)
SMEM = pl.BlockSpec(memory_space=pltpu.SMEM)


def params(mib=20):
    return pltpu.CompilerParams(vmem_limit_bytes=mib * 1024 * 1024)


def dot(a, b, ca, cb):
    return lax.dot_general(a, b, (((ca,), (cb,)), ((), ())), preferred_element_type=F32)


def iota(shape, axis):
    return lax.broadcasted_iota(jnp.int32, shape, axis)


def weight_pairs(m):
    pairs = []
    for c in range(NC):
        for h in range(NX):
            k = (h + m) % 2
            pairs.append((c * NX + h, (h // 2) * NX + 2 * c + k))
    return pairs


def select_x(at_ref, table_ref, x_ref, out_ref, pick_ref):
    ids = (NX * iota((PEER, TOK), 0) + at_ref[3]).astype(F32)
    before = (iota((TOK, TOK), 0) < iota((TOK, TOK), 1)).astype(BF)
    slot = (iota((ROWS, TOK), 0) % SLOT).astype(F32)
    lane = iota((ROWS, TOK), 1)
    table = table_ref[...]
    hit = jnp.zeros((PEER, TOK), F32)
    chance = jnp.zeros((PEER, TOK), F32)
    for k in range(TOP):
        on = table[k : k + 1, :] == ids
        hit = jnp.where(on, 1.0, hit)
        chance = jnp.where(on, table[TOP + k : TOP + k + 1, :], chance)
    rank = dot(hit.astype(BF), before, 1, 0)
    rank = jnp.where(hit > 0.5, rank, -1.0)
    rank = jnp.broadcast_to(rank[:, None, :], (PEER, SLOT, TOK)).reshape(ROWS, TOK)
    chance = jnp.broadcast_to(chance[:, None, :], (PEER, SLOT, TOK)).reshape(ROWS, TOK)
    mine = rank == slot
    share = jnp.sum(jnp.where(mine, chance, 0.0), axis=1, keepdims=True)
    pick = jnp.where(mine, 1.0, 0.0).astype(BF)
    pick_ref[...] = pick
    for h in range(NX):
        out_ref[:, h * Q : (h + 1) * Q] = dot(pick, x_ref[h], 1, 0).astype(BF)
    out_ref[:, D:] = jnp.where(lane == 0, share, 0.0).astype(BF)


def select_d(pick_ref, d_ref, out_ref):
    for h in range(NX):
        out_ref[:, h * Q : (h + 1) * Q] = dot(pick_ref[...], d_ref[h], 1, 0).astype(BF)


def both(wa_ref, wb_ref, i, h):
    cols = slice(h * Q, (h + 1) * Q)
    return jnp.concatenate([wa_ref[i, :, cols], wb_ref[i, :, cols]], axis=0)


def project(ref, wa_ref, wb_ref, i):
    total = dot(ref[:, :Q], both(wa_ref, wb_ref, i, 0), 1, 1)
    for h in range(1, NX):
        total = total + dot(ref[:, h * Q : (h + 1) * Q], both(wa_ref, wb_ref, i, h), 1, 1)
    return total


def gates(x_ref, wa_ref, wb_ref, pre_ref, keep_ref):
    weight = x_ref[:, D:].astype(F32)[:, :1]
    gate = project(x_ref, wa_ref, wb_ref, 0)
    up = project(x_ref, wa_ref, wb_ref, 1)
    sig = 1.0 / (1.0 + jnp.exp(-gate))
    act = gate * sig
    hidden = act * up
    pre_ref[0] = hidden
    pre_ref[1] = weight * (up * (sig * (1.0 + gate * (1.0 - sig))))
    pre_ref[2] = weight * act
    keep_ref[...] = (weight * hidden).astype(BF)


def expert(at_ref, pre_ref, d_ref, wa_ref, wb_ref, da_ref, db_ref, part_ref, keep_ref):
    raw = project(d_ref, da_ref, db_ref, 0)
    score = jnp.sum(pre_ref[0] * raw, axis=1, keepdims=True)
    keep_ref[0] = (raw * pre_ref[1]).astype(BF)
    keep_ref[1] = (raw * pre_ref[2]).astype(BF)
    for h in range(NX):
        total = dot(keep_ref[0], both(wa_ref, wb_ref, 0, h), 1, 0)
        total = total + dot(keep_ref[1], both(wa_ref, wb_ref, 1, h), 1, 0)
        part_ref[:, h * Q : (h + 1) * Q] = total.astype(BF)
    lane = iota((ROWS, TOK), 1) - 2 * at_ref[2]
    coarse = score.astype(BF).astype(F32)
    carried = jnp.where(lane == 0, coarse, jnp.where(lane == 1, score - coarse, 0.0))
    part_ref[:, D:] = carried.astype(BF)


def down_grads(do_ref, ds_ref, ho_ref, hs_ref, a_ref, b_ref, flip):
    @pl.when(pl.program_id(0) == 0)
    def _():
        flip[:, :ROWS] = ho_ref[...].T
        flip[:, ROWS:] = hs_ref[...].T

    grad = dot(flip[...], jnp.concatenate([do_ref[...], ds_ref[...]], axis=0), 1, 0).astype(BF)
    a_ref[0] = grad[:FQ]
    b_ref[0] = grad[FQ:]


def gate_up_grads(xo_ref, xs_ref, ko_ref, ks_ref, a_ref, b_ref, flip):
    @pl.when(pl.program_id(0) == 0)
    def _():
        for i in range(2):
            flip[i, :, :ROWS] = ko_ref[i].T
            flip[i, :, ROWS:] = ks_ref[i].T

    x = jnp.concatenate([xo_ref[...], xs_ref[...]], axis=0)
    for i in range(2):
        grad = dot(flip[i], x, 1, 0).astype(BF)
        a_ref[i] = grad[:FQ]
        b_ref[i] = grad[FQ:]


def place(at_ref, da_ref, db_ref, a_ref, b_ref, gate_ref, up_ref, down_ref):
    odd = at_ref[3] % 2
    for out, a, b in (
        (gate_ref, a_ref[0], b_ref[0]),
        (up_ref, a_ref[1], b_ref[1]),
        (down_ref, da_ref[0], db_ref[0]),
    ):
        out[odd] = a
        out[1 - odd] = b


def combine(at_ref, table_ref, pick_ref, home_ref, out_ref):
    ids = (NX * iota((PEER, TOK), 0) + at_ref[3]).astype(F32)
    pick = pick_ref[...]
    carried = home_ref[:, D:].astype(F32)
    score = (carried[:, 0:1] + carried[:, 1:2]) + (carried[:, 2:3] + carried[:, 3:4])
    spread = jnp.sum((pick.astype(F32) * score).reshape(PEER, SLOT, TOK), axis=1)
    table = table_ref[...]
    lines = [
        jnp.sum(jnp.where(table[k : k + 1, :] == ids, spread, 0.0), axis=0, keepdims=True) for k in range(TOP)
    ]
    lines = jnp.concatenate(lines + [jnp.zeros((16 - TOP, TOK), F32)], axis=0)
    coarse = lines.astype(BF)
    fine = (lines - coarse.astype(F32)).astype(BF)
    for h in range(NX):
        out_ref[h, :TOK, :] = dot(pick, home_ref[:, h * Q : (h + 1) * Q], 0, 0).astype(BF)
        out_ref[h, TOK:, :TOK] = coarse
        out_ref[h, TOK:, TOK : 2 * TOK] = fine
        out_ref[h, TOK:, 2 * TOK :] = jnp.zeros((16, Q - 2 * TOK), BF)


def per_device(tokens, cotangent, route, prob, w_gate, w_up, w_down):
    at = jnp.stack([lax.axis_index(a) for a in ("y", "z", "c", "x")]).astype(jnp.int32)
    ix = lax.axis_index("x")
    sib = [(0, 1), (1, 0)]
    shape = jax.ShapeDtypeStruct

    def to_experts(rows):
        rows = rows.reshape(PEER, SLOT, rows.shape[1])
        rows = lax.all_to_all(rows, ("y", "z"), split_axis=0, concat_axis=0, tiled=True)
        return rows.reshape(ROWS, rows.shape[2])

    with jax.named_scope("select_x"):
        xg = lax.all_gather(tokens, "x", axis=0, tiled=False)
        table = jnp.concatenate([route.T.astype(F32), prob.T.astype(F32)], axis=0)
        xs, pick = pl.pallas_call(
            select_x,
            out_shape=(shape((ROWS, WIDE), BF), shape((ROWS, TOK), BF)),
            in_specs=[SMEM, VMEM, VMEM],
            out_specs=(VMEM, VMEM),
            compiler_params=params(),
            name="select_x",
        )(at, table, xg)
        x_own = to_experts(xs)

    with jax.named_scope("select_d"):
        pick, cotangent = lax.optimization_barrier((pick, cotangent))
        dg = lax.all_gather(cotangent, "x", axis=0, tiled=False)

    with jax.named_scope("weights_out"):
        dg, *mats = lax.optimization_barrier((dg, w_gate, w_up, w_down))
        weights = []
        for m in (0, 1, 0, 1):
            k = (ix + m) % 2
            if len(weights) == 2:
                *mats, weights[1] = lax.optimization_barrier((*mats, weights[1]))
            which = mats[2:] if len(weights) > 1 else mats[:2]
            piece = jnp.stack([lax.dynamic_index_in_dim(w, k, 0, keepdims=False) for w in which])
            weights.append(lax.ppermute(piece, ("c", "x"), weight_pairs(m)))

    with jax.named_scope("select_d"):
        ds = pl.pallas_call(
            select_d,
            out_shape=shape((ROWS, D), BF),
            in_specs=[VMEM, VMEM],
            out_specs=VMEM,
            compiler_params=params(),
            name="select_d",
        )(pick, dg)

    with jax.named_scope("gates"):
        x_own, ds = lax.optimization_barrier((x_own, ds))
        d_own = to_experts(ds)
        x_sib = lax.ppermute(x_own, "c", sib)
        ahead = pl.pallas_call(
            gates,
            out_shape=(shape((3, ROWS, FH), F32), shape((ROWS, FH), BF)),
            in_specs=[VMEM] * 3,
            out_specs=(VMEM, VMEM),
            cost_estimate=pl.CostEstimate(flops=COST, bytes_accessed=COST // 100, transcendentals=0),
            compiler_params=params(),
            name="gates",
        )
        pre_own, hid_own = ahead(x_own, *weights[:2])
        pre_sib, hid_sib = ahead(x_sib, *weights[:2])
        pre_own, pre_sib, *weights = lax.optimization_barrier((pre_own, pre_sib, *weights))
        d_own, pre_own, pre_sib = lax.optimization_barrier((d_own, pre_own, pre_sib))

    with jax.named_scope("expert"):
        d_sib = lax.ppermute(d_own, "c", sib)
        run = pl.pallas_call(
            expert,
            out_shape=(shape((ROWS, WIDE), BF), shape((2, ROWS, FH), BF)),
            in_specs=[SMEM] + [VMEM] * 6,
            out_specs=(VMEM, VMEM),
            compiler_params=params(),
            name="expert",
        )
        part_own, keep_own = run(at, pre_own, d_own, *weights)
        part_own, d_sib = lax.optimization_barrier((part_own, d_sib))
        part_sib, keep_sib = run(at, pre_sib, d_sib, *weights)
        part_sib, hid_own, hid_sib = lax.optimization_barrier((part_sib, hid_own, hid_sib))
        sent = lax.ppermute(part_sib, "c", sib)

    with jax.named_scope("weights_back"):
        cut = pl.BlockSpec((ROWS, Q), lambda h: (0, h))
        h_spec = pl.BlockSpec((ROWS, FH), lambda h: (0, 0))
        k_spec = pl.BlockSpec((2, ROWS, FH), lambda h: (0, 0, 0))
        back = []

        def home_again(pieces):
            for m, piece in enumerate(pieces):
                back.append(lax.ppermute(piece, ("c", "x"), [(b, a) for a, b in weight_pairs(m)]))

        pieces = pl.pallas_call(
            down_grads,
            grid=(NX,),
            out_shape=(shape((1, FQ, D), BF),) * 2,
            in_specs=[cut, cut, h_spec, h_spec],
            out_specs=(pl.BlockSpec((1, FQ, Q), lambda h: (0, 0, h)),) * 2,
            scratch_shapes=[pltpu.VMEM((FH, 2 * ROWS), BF)],
            compiler_params=params(),
            name="down_grads",
        )(d_own, d_sib, hid_own, hid_sib)
        *pieces, sent = lax.optimization_barrier((*pieces, sent))
        home_again(pieces)
        total = (part_own.astype(F32) + sent.astype(F32)).astype(BF)
        total, keep_own, keep_sib = lax.optimization_barrier((total, keep_own, keep_sib))
        back[0], back[1], keep_own, keep_sib = lax.optimization_barrier((back[0], back[1], keep_own, keep_sib))
        pieces = pl.pallas_call(
            gate_up_grads,
            grid=(NX,),
            out_shape=(shape((2, FQ, D), BF),) * 2,
            in_specs=[cut, cut, k_spec, k_spec],
            out_specs=(pl.BlockSpec((2, FQ, Q), lambda h: (0, 0, h)),) * 2,
            scratch_shapes=[pltpu.VMEM((2, FH, 2 * ROWS), BF)],
            cost_estimate=pl.CostEstimate(flops=COST, bytes_accessed=COST // 100, transcendentals=0),
            compiler_params=params(60),
            name="gate_up_grads",
        )(x_own, x_sib, keep_own, keep_sib)
        home_again(pieces)
        part_rows = FQ // 4
        grad_gate, grad_up, grad_down = pl.pallas_call(
            place,
            grid=(4,),
            out_shape=(shape((2, FQ, D), BF),) * 3,
            in_specs=[SMEM] + [pl.BlockSpec((n, part_rows, D), lambda i: (0, i, 0)) for n in (1, 1, 2, 2)],
            out_specs=(pl.BlockSpec((2, part_rows, D), lambda i: (0, i, 0)),) * 3,
            compiler_params=params(),
            name="place",
        )(at, *back)

    with jax.named_scope("tokens_back"):
        home = to_experts(total)
        partial = pl.pallas_call(
            combine,
            out_shape=shape((NX, TOK + 16, Q), BF),
            in_specs=[SMEM, VMEM, VMEM, VMEM],
            out_specs=VMEM,
            compiler_params=params(),
            name="combine",
        )(at, table, pick, home)
        last = lax.all_to_all(partial, "x", split_axis=0, concat_axis=0, tiled=True).astype(F32)
        grad_tokens = jnp.sum(last[:, :TOK], axis=0).astype(BF)
        lines = jnp.sum(last[:, TOK : TOK + TOP, : 2 * TOK], axis=0)
        grad_prob = (lines[:, :TOK] + lines[:, TOK:]).T
    return (grad_tokens, grad_prob, grad_gate, grad_up, grad_down)


def solution(mesh):
    grid = Mesh(mesh.devices.reshape(NY, NZ, NC, NX), ("y", "z", "c", "x"))
    owner = ("y", "z", "c")
    wide = P(owner, "x")
    thin = P(owner, None)
    deep = P(owner, "x", None)
    return jax.shard_map(
        per_device,
        mesh=grid,
        in_specs=(wide, wide, thin, thin, deep, deep, deep),
        out_specs=(wide, thin, deep, deep, deep),
        check_vma=False,
    )
```

```python
import jax
import jax.numpy as jnp
from jax import lax
from jax.experimental import pallas as pl
from jax.experimental.pallas import tpu as pltpu
from jax.sharding import Mesh, PartitionSpec as P

BF = jnp.bfloat16
F32 = jnp.float32
NY, NZ, NC, NX = 4, 8, 2, 4
SLOT = 16
TOK = 128
TOP = 8
PEER = NY * NZ
ROWS = PEER * SLOT
Q = 512
D = NX * Q
WIDE = D + 128
FQ = 192
FH = 2 * FQ
COST = 100_000_000_000
VMEM = pl.BlockSpec(memory_space=pltpu.VMEM)
SMEM = pl.BlockSpec(memory_space=pltpu.SMEM)


def params(mib=20):
    return pltpu.CompilerParams(vmem_limit_bytes=mib * 1024 * 1024)


def dot(a, b, ca, cb):
    return lax.dot_general(a, b, (((ca,), (cb,)), ((), ())), preferred_element_type=F32)


def iota(shape, axis):
    return lax.broadcasted_iota(jnp.int32, shape, axis)


def weight_pairs(m):
    pairs = []
    for c in range(NC):
        for h in range(NX):
            k = (h + m) % 2
            pairs.append((c * NX + h, (h // 2) * NX + 2 * c + k))
    return pairs


def select_x(at_ref, table_ref, x_ref, out_ref, pick_ref):
    ids = (NX * iota((PEER, TOK), 0) + at_ref[3]).astype(F32)
    before = (iota((TOK, TOK), 0) < iota((TOK, TOK), 1)).astype(BF)
    slot = (iota((ROWS, TOK), 0) % SLOT).astype(F32)
    lane = iota((ROWS, TOK), 1)
    table = table_ref[...]
    hit = jnp.zeros((PEER, TOK), F32)
    chance = jnp.zeros((PEER, TOK), F32)
    for k in range(TOP):
        on = table[k : k + 1, :] == ids
        hit = jnp.where(on, 1.0, hit)
        chance = jnp.where(on, table[TOP + k : TOP + k + 1, :], chance)
    rank = dot(hit.astype(BF), before, 1, 0)
    rank = jnp.where(hit > 0.5, rank, -1.0)
    rank = jnp.broadcast_to(rank[:, None, :], (PEER, SLOT, TOK)).reshape(ROWS, TOK)
    chance = jnp.broadcast_to(chance[:, None, :], (PEER, SLOT, TOK)).reshape(ROWS, TOK)
    mine = rank == slot
    share = jnp.sum(jnp.where(mine, chance, 0.0), axis=1, keepdims=True)
    pick = jnp.where(mine, 1.0, 0.0).astype(BF)
    pick_ref[...] = pick
    for h in range(NX):
        out_ref[:, h * Q : (h + 1) * Q] = dot(pick, x_ref[h], 1, 0).astype(BF)
    out_ref[:, D:] = jnp.where(lane == 0, share, 0.0).astype(BF)


def select_d(pick_ref, d_ref, out_ref):
    for h in range(NX):
        out_ref[:, h * Q : (h + 1) * Q] = dot(pick_ref[...], d_ref[h], 1, 0).astype(BF)


def both(wa_ref, wb_ref, i, h):
    cols = slice(h * Q, (h + 1) * Q)
    return jnp.concatenate([wa_ref[i, :, cols], wb_ref[i, :, cols]], axis=0)


def project(ref, wa_ref, wb_ref, i):
    total = dot(ref[:, :Q], both(wa_ref, wb_ref, i, 0), 1, 1)
    for h in range(1, NX):
        total = total + dot(ref[:, h * Q : (h + 1) * Q], both(wa_ref, wb_ref, i, h), 1, 1)
    return total


def gates(x_ref, wa_ref, wb_ref, pre_ref, keep_ref):
    weight = x_ref[:, D:].astype(F32)[:, :1]
    gate = project(x_ref, wa_ref, wb_ref, 0)
    up = project(x_ref, wa_ref, wb_ref, 1)
    sig = 1.0 / (1.0 + jnp.exp(-gate))
    act = gate * sig
    hidden = act * up
    pre_ref[0] = hidden
    pre_ref[1] = weight * (up * (sig * (1.0 + gate * (1.0 - sig))))
    pre_ref[2] = weight * act
    keep_ref[...] = (weight * hidden).astype(BF)


def expert(at_ref, pre_ref, d_ref, wa_ref, wb_ref, da_ref, db_ref, part_ref, keep_ref):
    raw = project(d_ref, da_ref, db_ref, 0)
    score = jnp.sum(pre_ref[0] * raw, axis=1, keepdims=True)
    keep_ref[0] = (raw * pre_ref[1]).astype(BF)
    keep_ref[1] = (raw * pre_ref[2]).astype(BF)
    for h in range(NX):
        total = dot(keep_ref[0], both(wa_ref, wb_ref, 0, h), 1, 0)
        total = total + dot(keep_ref[1], both(wa_ref, wb_ref, 1, h), 1, 0)
        part_ref[:, h * Q : (h + 1) * Q] = total.astype(BF)
    lane = iota((ROWS, TOK), 1) - 2 * at_ref[2]
    coarse = score.astype(BF).astype(F32)
    carried = jnp.where(lane == 0, coarse, jnp.where(lane == 1, score - coarse, 0.0))
    part_ref[:, D:] = carried.astype(BF)


def down_grads(do_ref, ds_ref, ho_ref, hs_ref, a_ref, b_ref, flip):
    @pl.when(pl.program_id(0) == 0)
    def _():
        flip[:, :ROWS] = ho_ref[...].T
        flip[:, ROWS:] = hs_ref[...].T

    grad = dot(flip[...], jnp.concatenate([do_ref[...], ds_ref[...]], axis=0), 1, 0).astype(BF)
    a_ref[0] = grad[:FQ]
    b_ref[0] = grad[FQ:]


def gate_up_grads(xo_ref, xs_ref, ko_ref, ks_ref, a_ref, b_ref, flip):
    @pl.when(pl.program_id(0) == 0)
    def _():
        for i in range(2):
            flip[i, :, :ROWS] = ko_ref[i].T
            flip[i, :, ROWS:] = ks_ref[i].T

    x = jnp.concatenate([xo_ref[...], xs_ref[...]], axis=0)
    for i in range(2):
        grad = dot(flip[i], x, 1, 0).astype(BF)
        a_ref[i] = grad[:FQ]
        b_ref[i] = grad[FQ:]


def place(at_ref, da_ref, db_ref, a_ref, b_ref, gate_ref, up_ref, down_ref):
    odd = at_ref[3] % 2
    for out, a, b in (
        (gate_ref, a_ref[0], b_ref[0]),
        (up_ref, a_ref[1], b_ref[1]),
        (down_ref, da_ref[0], db_ref[0]),
    ):
        out[odd] = a
        out[1 - odd] = b


def combine(at_ref, table_ref, pick_ref, home_ref, out_ref):
    ids = (NX * iota((PEER, TOK), 0) + at_ref[3]).astype(F32)
    pick = pick_ref[...]
    carried = home_ref[:, D:].astype(F32)
    score = (carried[:, 0:1] + carried[:, 1:2]) + (carried[:, 2:3] + carried[:, 3:4])
    spread = jnp.sum((pick.astype(F32) * score).reshape(PEER, SLOT, TOK), axis=1)
    table = table_ref[...]
    lines = [
        jnp.sum(jnp.where(table[k : k + 1, :] == ids, spread, 0.0), axis=0, keepdims=True) for k in range(TOP)
    ]
    lines = jnp.concatenate(lines + [jnp.zeros((16 - TOP, TOK), F32)], axis=0)
    coarse = lines.astype(BF)
    fine = (lines - coarse.astype(F32)).astype(BF)
    for h in range(NX):
        out_ref[h, :TOK, :] = dot(pick, home_ref[:, h * Q : (h + 1) * Q], 0, 0).astype(BF)
        out_ref[h, TOK:, :TOK] = coarse
        out_ref[h, TOK:, TOK : 2 * TOK] = fine
        out_ref[h, TOK:, 2 * TOK :] = jnp.zeros((16, Q - 2 * TOK), BF)


def per_device(tokens, cotangent, route, prob, w_gate, w_up, w_down):
    at = jnp.stack([lax.axis_index(a) for a in ("y", "z", "c", "x")]).astype(jnp.int32)
    ix = lax.axis_index("x")
    sib = [(0, 1), (1, 0)]
    shape = jax.ShapeDtypeStruct

    def to_experts(rows):
        rows = rows.reshape(PEER, SLOT, rows.shape[1])
        rows = lax.all_to_all(rows, ("y", "z"), split_axis=0, concat_axis=0, tiled=True)
        return rows.reshape(ROWS, rows.shape[2])

    with jax.named_scope("select_x"):
        xg = lax.all_gather(tokens, "x", axis=0, tiled=False)
        table = jnp.concatenate([route.T.astype(F32), prob.T.astype(F32)], axis=0)
        xs, pick = pl.pallas_call(
            select_x,
            out_shape=(shape((ROWS, WIDE), BF), shape((ROWS, TOK), BF)),
            in_specs=[SMEM, VMEM, VMEM],
            out_specs=(VMEM, VMEM),
            compiler_params=params(),
            name="select_x",
        )(at, table, xg)
        x_own = to_experts(xs)

    with jax.named_scope("select_d"):
        pick, cotangent = lax.optimization_barrier((pick, cotangent))
        dg = lax.all_gather(cotangent, "x", axis=0, tiled=False)

    with jax.named_scope("weights_out"):
        dg, *mats = lax.optimization_barrier((dg, w_gate, w_up, w_down))
        weights = []
        for m in (0, 1, 0, 1):
            k = (ix + m) % 2
            which = mats[2:] if len(weights) > 1 else mats[:2]
            piece = jnp.stack([lax.dynamic_index_in_dim(w, k, 0, keepdims=False) for w in which])
            weights.append(lax.ppermute(piece, ("c", "x"), weight_pairs(m)))

    with jax.named_scope("select_d"):
        ds = pl.pallas_call(
            select_d,
            out_shape=shape((ROWS, D), BF),
            in_specs=[VMEM, VMEM],
            out_specs=VMEM,
            compiler_params=params(),
            name="select_d",
        )(pick, dg)

    with jax.named_scope("gates"):
        x_own, ds = lax.optimization_barrier((x_own, ds))
        d_own = to_experts(ds)
        x_sib = lax.ppermute(x_own, "c", sib)
        ahead = pl.pallas_call(
            gates,
            out_shape=(shape((3, ROWS, FH), F32), shape((ROWS, FH), BF)),
            in_specs=[VMEM] * 3,
            out_specs=(VMEM, VMEM),
            cost_estimate=pl.CostEstimate(flops=COST, bytes_accessed=COST // 100, transcendentals=0),
            compiler_params=params(),
            name="gates",
        )
        pre_own, hid_own = ahead(x_own, *weights[:2])
        pre_sib, hid_sib = ahead(x_sib, *weights[:2])
        pre_own, pre_sib, *weights = lax.optimization_barrier((pre_own, pre_sib, *weights))
        d_own, pre_own, pre_sib = lax.optimization_barrier((d_own, pre_own, pre_sib))

    with jax.named_scope("expert"):
        d_sib = lax.ppermute(d_own, "c", sib)
        run = pl.pallas_call(
            expert,
            out_shape=(shape((ROWS, WIDE), BF), shape((2, ROWS, FH), BF)),
            in_specs=[SMEM] + [VMEM] * 6,
            out_specs=(VMEM, VMEM),
            compiler_params=params(),
            name="expert",
        )
        part_own, keep_own = run(at, pre_own, d_own, *weights)
        part_own, d_sib = lax.optimization_barrier((part_own, d_sib))
        part_sib, keep_sib = run(at, pre_sib, d_sib, *weights)
        part_sib, hid_own, hid_sib = lax.optimization_barrier((part_sib, hid_own, hid_sib))
        sent = lax.ppermute(part_sib, "c", sib)

    with jax.named_scope("weights_back"):
        cut = pl.BlockSpec((ROWS, Q), lambda h: (0, h))
        h_spec = pl.BlockSpec((ROWS, FH), lambda h: (0, 0))
        k_spec = pl.BlockSpec((2, ROWS, FH), lambda h: (0, 0, 0))
        back = []

        def home_again(pieces):
            for m, piece in enumerate(pieces):
                back.append(lax.ppermute(piece, ("c", "x"), [(b, a) for a, b in weight_pairs(m)]))

        pieces = pl.pallas_call(
            down_grads,
            grid=(NX,),
            out_shape=(shape((1, FQ, D), BF),) * 2,
            in_specs=[cut, cut, h_spec, h_spec],
            out_specs=(pl.BlockSpec((1, FQ, Q), lambda h: (0, 0, h)),) * 2,
            scratch_shapes=[pltpu.VMEM((FH, 2 * ROWS), BF)],
            compiler_params=params(),
            name="down_grads",
        )(d_own, d_sib, hid_own, hid_sib)
        *pieces, sent = lax.optimization_barrier((*pieces, sent))
        home_again(pieces)
        total = (part_own.astype(F32) + sent.astype(F32)).astype(BF)
        total, keep_own, keep_sib = lax.optimization_barrier((total, keep_own, keep_sib))
        back[0], back[1], keep_own, keep_sib = lax.optimization_barrier((back[0], back[1], keep_own, keep_sib))
        pieces = pl.pallas_call(
            gate_up_grads,
            grid=(NX,),
            out_shape=(shape((2, FQ, D), BF),) * 2,
            in_specs=[cut, cut, k_spec, k_spec],
            out_specs=(pl.BlockSpec((2, FQ, Q), lambda h: (0, 0, h)),) * 2,
            scratch_shapes=[pltpu.VMEM((2, FH, 2 * ROWS), BF)],
            cost_estimate=pl.CostEstimate(flops=COST, bytes_accessed=COST // 100, transcendentals=0),
            compiler_params=params(60),
            name="gate_up_grads",
        )(x_own, x_sib, keep_own, keep_sib)
        home_again(pieces)
        part_rows = FQ // 4
        grad_gate, grad_up, grad_down = pl.pallas_call(
            place,
            grid=(4,),
            out_shape=(shape((2, FQ, D), BF),) * 3,
            in_specs=[SMEM] + [pl.BlockSpec((n, part_rows, D), lambda i: (0, i, 0)) for n in (1, 1, 2, 2)],
            out_specs=(pl.BlockSpec((2, part_rows, D), lambda i: (0, i, 0)),) * 3,
            compiler_params=params(),
            name="place",
        )(at, *back)

    with jax.named_scope("tokens_back"):
        home = to_experts(total)
        partial = pl.pallas_call(
            combine,
            out_shape=shape((NX, TOK + 16, Q), BF),
            in_specs=[SMEM, VMEM, VMEM, VMEM],
            out_specs=VMEM,
            compiler_params=params(),
            name="combine",
        )(at, table, pick, home)
        last = lax.all_to_all(partial, "x", split_axis=0, concat_axis=0, tiled=True).astype(F32)
        grad_tokens = jnp.sum(last[:, :TOK], axis=0).astype(BF)
        lines = jnp.sum(last[:, TOK : TOK + TOP, : 2 * TOK], axis=0)
        grad_prob = (lines[:, :TOK] + lines[:, TOK:]).T
    return (grad_tokens, grad_prob, grad_gate, grad_up, grad_down)


def solution(mesh):
    grid = Mesh(mesh.devices.reshape(NY, NZ, NC, NX), ("y", "z", "c", "x"))
    owner = ("y", "z", "c")
    wide = P(owner, "x")
    thin = P(owner, None)
    deep = P(owner, "x", None)
    return jax.shard_map(
        per_device,
        mesh=grid,
        in_specs=(wide, wide, thin, thin, deep, deep, deep),
        out_specs=(wide, thin, deep, deep, deep),
        check_vma=False,
    )
```
